32 devices in a mesh: groups: 2 (over y), seq: 4 (over z), head: 4 (over x, core).
Axes of the slice: x: 2, y: 2, z: 4, core: 2. Of those that a mesh axis runs over, the one named last changes fastest.
Arguments:
- hidden: bfloat16 [2048, 2560], P(('groups', 'seq'), 'head'), parts along dimension 0, may hold values from -6 to 6
- w_zx: bfloat16 [2560, 2, 3072], P('seq', None, 'head'), may hold values from -0.125 to 0.125
- w_dt: bfloat16 [2560, 48], P('seq', 'head'), may hold values from -0.125 to 0.125
- w_bc: bfloat16 [2560, 2, 128], P('seq'), may hold values from -0.125 to 0.125
- dt_bias: float32 [48], P('head'), may hold values from -1 to 0
- a_log: float32 [48], P('head'), may hold values from -12 to -2, as said below
- d_skip: float32 [48], P('head'), may hold values from 0.5 to 1.5
- norm_gain: float32 [3072], P('head'), may hold values from 0.5 to 1.5
- w_out: bfloat16 [3072, 2560], P('head', 'seq'), may hold values from -0.109375 to 0.109375
- grad_out: bfloat16 [2048, 2560], P(('groups', 'seq'), 'head'), parts along dimension 0, may hold values from -6 to 6
Outputs:
- layer_out: bfloat16 [2048, 2560], P(('groups', 'seq'), 'head'), parts along dimension 0
- grad_hidden: bfloat16 [2048, 2560], P(('groups', 'seq'), 'head'), parts along dimension 0
- grad_wzx: float32 [5120, 2, 3072], P(('groups', 'seq'), None, 'head'), parts along dimension 0
- grad_wdt: float32 [5120, 48], P(('groups', 'seq'), 'head'), parts along dimension 0
- grad_wbc: float32 [5120, 2, 128], P(('groups', 'seq')), parts along dimension 0
- grad_dtbias: float32 [96], P(('groups', 'head')), parts along dimension 0
- grad_alog: float32 [96], P(('groups', 'head')), parts along dimension 0
- grad_dskip: float32 [96], P(('groups', 'head')), parts along dimension 0
- grad_gain: float32 [6144], P(('groups', 'head')), parts along dimension 0
- grad_wout: float32 [6144, 2560], P(('groups', 'head'), 'seq'), parts along dimension 0
The draws below stay inside these ranges and needn't reach their ends.
There are 2 independent parts, one for each index of `groups`. The reference program is written for one: setup_inputs(seed, part) draws one part's arguments, and reference() takes and returns one part's arrays. A program takes and returns all parts, laid end to end along the dimension named above; an argument that names none is the same for every part. Nothing has to cross between parts.
Inputs may be any that keep to these rules, and one draw needn't show every extreme that they name: `a_log`: log of each head's decay rate.
All inputs are finite; a program needn't handle non-finite values.
Results may differ from the reference program's by a relative error of at most 0.029.
Values may be sent and summed in bfloat16 or wider, within the bound.
No kernel may reach another device: no remote copies, remote signals or barrier semaphores. Data moves between devices by JAX's collectives and lax.ppermute only.
A program may use at most 128 MiB of HBM per device.

```python
import jax
import jax.numpy as jnp
from jax import lax

D = 2560
HEADS = 48
HDIM = 64
STATE = 128
BLOCK = 128
L_DEV = 256
SEQLEN = 1024
DI = 3072
N_SEQ = 4
N_HEAD = 4


def draw_a_log(key, part):
    pick_key, slow_key, fast_key = jax.random.split(jax.random.fold_in(key, 17), 3)
    share = 0.5
    slow_mask = jax.random.uniform(pick_key, (HEADS,)) < share
    slow_rate = jnp.exp(jax.random.uniform(slow_key, (HEADS,), minval=jnp.log(0.8 / SEQLEN), maxval=jnp.log(2.0 / SEQLEN)))
    fast_rate = jnp.exp(jax.random.uniform(fast_key, (HEADS,), minval=jnp.log(1.0 / 50.0), maxval=jnp.log(1.0 / 30.0)))
    return jnp.log(jnp.where(slow_mask, slow_rate, fast_rate) / 0.6).astype(jnp.float32)


def steps_of(stream_key, dims, cuts, low, top_value):
    level = 1.0
    for axis_at, blocks in cuts:
        steps = jax.random.uniform(jax.random.fold_in(jax.random.fold_in(stream_key, 6), axis_at), (blocks,), jnp.float32, low / len(cuts), top_value / len(cuts))
        level = level * jnp.repeat(jnp.exp(steps), dims[axis_at] // blocks).reshape((-1,) + (1,) * (len(dims) - 1 - axis_at))
    return level


def bell_draw(key, extent, deviation, most, pieces=(), kind=jnp.bfloat16):
    array = jax.random.normal(key, extent, jnp.float32) * deviation
    if len(pieces) > 0:
        array = steps_of(key, extent, pieces, -0.22, 0.18) * array
    return jnp.clip(array, min=-most, max=most).astype(kind)


def setup_inputs(seed: int = 0, part: int = 0) -> dict:
    keys = jax.random.split(jax.random.key(seed), 11)
    part_keys = jax.random.split(jax.random.fold_in(keys[10], part), 11)
    hidden = bell_draw(part_keys[0], (SEQLEN, D), 1.0, 6.0, ((0, 4), (1, 4)))
    w_zx = bell_draw(keys[1], (D, 2, DI), D ** -0.5, 0.125, ((0, 4), (2, 4)))
    w_dt = bell_draw(keys[2], (D, HEADS), D ** -0.5, 0.125, ((0, 4), (1, 4)))
    w_bc = bell_draw(keys[3], (D, 2, STATE), D ** -0.5, 0.125, ((0, 4),))
    dt_bias = jnp.clip(-1.0 + 1.0 * jax.random.uniform(keys[4], (HEADS,), jnp.float32) ** steps_of(keys[4], (HEADS,), ((0, 4),), -0.2, 0.2), -1.0, 0.0)
    a_log = draw_a_log(jax.random.fold_in(keys[10], 71), part)
    d_skip = jnp.clip(0.5 + 1.0 * jax.random.uniform(keys[6], (HEADS,), jnp.float32) ** steps_of(keys[6], (HEADS,), ((0, 4),), -0.2, 0.2), 0.5, 1.5)
    norm_gain = jnp.clip(1.0 + 0.1 * jax.random.normal(keys[7], (DI,), jnp.float32), 0.5, 1.5)
    w_out = bell_draw(keys[8], (DI, D), DI ** -0.5, 0.109375, ((0, 4), (1, 4)))
    grad_out = bell_draw(part_keys[9], (SEQLEN, D), 1.0, 6.0, ((0, 4), (1, 4)))
    return dict(hidden=hidden, w_zx=w_zx, w_dt=w_dt, w_bc=w_bc, dt_bias=dt_bias, a_log=a_log, d_skip=d_skip, norm_gain=norm_gain, w_out=w_out, grad_out=grad_out)


EPS_NORM = 1e-05
HIGH = lax.Precision.HIGHEST

def split_inputs(zx_f, dtr_f, bc_f, dt_bias, a_log):
    rows = dtr_f.shape[0]
    nheads = dtr_f.shape[1]
    width = zx_f.shape[2] // nheads
    z_gate = zx_f[:, 0]
    x_in = jax.nn.silu(zx_f[:, 1]).reshape(rows, nheads, width)
    dt_val = jax.nn.softplus(dtr_f + dt_bias[None])
    log_decay = -dt_val * jnp.exp(a_log)[None]
    return (z_gate, x_in, dt_val, log_decay, bc_f[:, 0], bc_f[:, 1])

def ssd_pass(x_in, dt_val, log_decay, b_in, c_in, d_skip, s_init, with_out):
    rows, nheads, width = x_in.shape
    blocks = rows // BLOCK
    lower = jnp.arange(BLOCK)[:, None] >= jnp.arange(BLOCK)[None, :]
    parts = (x_in.reshape(blocks, BLOCK, nheads, width), dt_val.reshape(blocks, BLOCK, nheads), log_decay.reshape(blocks, BLOCK, nheads), b_in.reshape(blocks, BLOCK, -1), c_in.reshape(blocks, BLOCK, -1))

    def advance(state, block):
        x_blk, dt_blk, ld_blk, b_blk, c_blk = block
        cumul = jnp.cumsum(ld_blk, axis=0)
        tail = cumul[-1]
        inflow = jnp.exp(tail[None] - cumul) * dt_blk
        fresh = state * jnp.exp(tail)[:, None, None] + jnp.einsum('sh,shp,sn->hpn', inflow, x_blk, b_blk, precision=HIGH)
        if not with_out:
            return (fresh, None)
        scores = jnp.dot(c_blk, b_blk.T, precision=HIGH)
        gaps = cumul.T[:, :, None] - cumul.T[:, None, :]
        weights = jnp.exp(jnp.where(lower[None], gaps, -1e+30)) * scores[None] * dt_blk.T[:, None, :]
        y_blk = jnp.einsum('hts,shp->thp', weights, x_blk, precision=HIGH)
        y_blk = y_blk + jnp.einsum('tn,hpn->thp', c_blk, state, precision=HIGH) * jnp.exp(cumul)[:, :, None]
        y_blk = y_blk + d_skip[None, :, None] * x_blk
        return (fresh, y_blk)
    final, outs = lax.scan(advance, s_init, parts)
    return (outs, final)

def mixer(zx_f, dtr_f, bc_f, dt_bias, a_log, d_skip, s_init):
    z_gate, x_in, dt_val, log_decay, b_in, c_in = split_inputs(zx_f, dtr_f, bc_f, dt_bias, a_log)
    outs, final = ssd_pass(x_in, dt_val, log_decay, b_in, c_in, d_skip, s_init, True)
    return outs.reshape(z_gate.shape[0], -1) * jax.nn.silu(z_gate)

def core(zx_f, dtr_f, bc_f, dt_bias, a_log, d_skip, norm_gain):
    start_state = jnp.zeros((dt_bias.shape[0], HDIM, STATE), zx_f.dtype)
    mixed = mixer(zx_f, dtr_f, bc_f, dt_bias, a_log, d_skip, start_state)
    rinv = lax.rsqrt(lax.optimization_barrier(jnp.mean(mixed * mixed, axis=1)) + EPS_NORM)
    return (mixed * rinv[:, None] * norm_gain[None]).astype(jnp.bfloat16)

def rounded(value):
    return lax.optimization_barrier(value.astype(jnp.bfloat16)).astype(jnp.float32)

def split_pair(value):
    upper = value.astype(jnp.bfloat16)
    lower_part = (value - upper.astype(value.dtype)).astype(jnp.bfloat16)
    return (upper, lower_part)

def reference(hidden, w_zx, w_dt, w_bc, dt_bias, a_log, d_skip, norm_gain, w_out, grad_out):
    total = hidden.shape[0]
    wide = HEADS * HDIM
    zx_b = jnp.dot(hidden, w_zx.reshape(D, 2 * wide), preferred_element_type=jnp.float32).astype(jnp.bfloat16)
    dtr_b = jnp.dot(hidden, w_dt, preferred_element_type=jnp.float32).astype(jnp.bfloat16)
    bc_b = jnp.dot(hidden, w_bc.reshape(D, 2 * STATE), preferred_element_type=jnp.float32).astype(jnp.bfloat16)
    zx_b, dtr_b, bc_b = lax.optimization_barrier((zx_b, dtr_b, bc_b))
    zx_f = zx_b.astype(jnp.float32).reshape(total, 2, wide)
    dtr_f = dtr_b.astype(jnp.float32)
    bc_f = bc_b.astype(jnp.float32).reshape(total, 2, STATE)
    gated, pull = jax.vjp(core, zx_f, dtr_f, bc_f, dt_bias, a_log, d_skip, norm_gain)
    group = wide // N_HEAD
    layer_sum = jnp.zeros((total, D), jnp.float32)
    for index in range(N_HEAD):
        part = jnp.dot(gated[:, index * group:(index + 1) * group], w_out[index * group:(index + 1) * group], preferred_element_type=jnp.float32)
        layer_sum = layer_sum + rounded(part)
    layer_out = layer_sum.astype(jnp.bfloat16)
    grad_gated = jnp.dot(grad_out, w_out.T, preferred_element_type=jnp.float32).astype(jnp.bfloat16)
    d_zx, d_dtr, d_bc, grad_dtbias, grad_alog, grad_dskip, grad_gain = pull(grad_gated)
    d_zx = d_zx.reshape(total, 2 * wide).astype(jnp.bfloat16)
    d_dtr = d_dtr.astype(jnp.bfloat16)
    d_bc = d_bc.reshape(total, 2 * STATE)
    bc_upper, bc_lower = split_pair(d_bc)
    flat_bc = w_bc.reshape(D, 2 * STATE)
    grad_hidden = (jnp.dot(d_zx, w_zx.reshape(D, 2 * wide).T, preferred_element_type=jnp.float32) + jnp.dot(d_dtr, w_dt.T, preferred_element_type=jnp.float32) + jnp.dot(bc_upper, flat_bc.T, preferred_element_type=jnp.float32) + jnp.dot(bc_lower, flat_bc.T, preferred_element_type=jnp.float32)).astype(jnp.bfloat16)

    def accumulate(index, sums):
        begin = index * L_DEV
        h_s = lax.dynamic_slice_in_dim(hidden, begin, L_DEV, 0)
        zx_s = lax.dynamic_slice_in_dim(d_zx, begin, L_DEV, 0)
        dt_s = lax.dynamic_slice_in_dim(d_dtr, begin, L_DEV, 0)
        hi_s = lax.dynamic_slice_in_dim(bc_upper, begin, L_DEV, 0)
        lo_s = lax.dynamic_slice_in_dim(bc_lower, begin, L_DEV, 0)
        g_s = lax.dynamic_slice_in_dim(gated, begin, L_DEV, 0)
        o_s = lax.dynamic_slice_in_dim(grad_out, begin, L_DEV, 0)
        bc_term = jnp.dot(h_s.T, hi_s, preferred_element_type=jnp.float32) + jnp.dot(h_s.T, lo_s, preferred_element_type=jnp.float32)
        return (sums[0] + rounded(jnp.dot(h_s.T, zx_s, preferred_element_type=jnp.float32)), sums[1] + rounded(jnp.dot(h_s.T, dt_s, preferred_element_type=jnp.float32)), sums[2] + rounded(bc_term), sums[3] + rounded(jnp.dot(g_s.T, o_s, preferred_element_type=jnp.float32)))
    start = (jnp.zeros((D, 2 * wide), jnp.float32), jnp.zeros((D, HEADS), jnp.float32), jnp.zeros((D, 2 * STATE), jnp.float32), jnp.zeros((wide, D), jnp.float32))
    grad_wzx, grad_wdt, grad_wbc, grad_wout = lax.fori_loop(0, N_SEQ, accumulate, start)
    return (layer_out, grad_hidden, grad_wzx.reshape(D, 2, wide), grad_wdt, grad_wbc.reshape(D, 2, STATE), grad_dtbias, grad_alog, grad_dskip, grad_gain, grad_wout)
```

```python
import jax
import jax.numpy as jnp
from jax import lax
from jax.sharding import PartitionSpec as P

HEADS = 48
HDIM = 64
BLOCK = 128


EPS_NORM = 1e-05
HIGH = lax.Precision.HIGHEST


def entering(x, axis, combine, identity):
    peers, here = (lax.axis_size(axis), lax.axis_index(axis))
    everything = jax.tree.map(
        lambda part, kind: lax.all_gather(part.astype(kind), axis), x, (jnp.bfloat16, jnp.bfloat16)
    )
    start = jax.tree.map(
        lambda part, zero: jnp.broadcast_to(jnp.asarray(zero, part.dtype), part.shape), x, identity
    )

    def entering_lap(k, before):
        reached = k < here
        new = combine(
            before, jax.tree.map(lambda part, own: part[k].astype(own.dtype), everything, x)
        )
        return jax.tree.map(lambda a, b: jnp.where(reached, a, b), new, before)

    return lax.fori_loop(0, peers, entering_lap, start)


def carried_in(x, axis, combine, identity):
    peers, here = (lax.axis_size(axis), lax.axis_index(axis))
    everything = jax.tree.map(
        lambda part, kind: lax.all_gather(part.astype(kind), axis),
        x,
        jax.tree.map(lambda a: jnp.bfloat16 if a.dtype == jnp.float32 else a.dtype, x),
    )
    start = jax.tree.map(
        lambda part, zero: jnp.broadcast_to(jnp.asarray(zero, part.dtype), part.shape), x, identity
    )

    def carried_lap(k, before):
        at = peers - 1 - k
        reached = at > here
        new = combine(
            before, jax.tree.map(lambda part, own: part[at].astype(own.dtype), everything, x)
        )
        return jax.tree.map(lambda a, b: jnp.where(reached, a, b), new, before)

    return lax.fori_loop(0, peers, carried_lap, start)


def split_inputs(zx_f, dtr_f, bc_f, dt_bias, a_log):
    rows = dtr_f.shape[0]
    nheads = dtr_f.shape[1]
    width = zx_f.shape[2] // nheads
    z_gate = zx_f[:, 0]
    x_in = jax.nn.silu(zx_f[:, 1]).reshape(rows, nheads, width)
    dt_val = jax.nn.softplus(dtr_f + dt_bias[None])
    log_decay = -dt_val * jnp.exp(a_log)[None]
    return (z_gate, x_in, dt_val, log_decay, bc_f[:, 0], bc_f[:, 1])


def ssd_pass(x_in, dt_val, log_decay, b_in, c_in, d_skip, s_init, with_out):
    rows, nheads, width = x_in.shape
    blocks = rows // BLOCK
    lower = jnp.arange(BLOCK)[:, None] >= jnp.arange(BLOCK)[None, :]
    parts = (
        x_in.reshape(blocks, BLOCK, nheads, width),
        dt_val.reshape(blocks, BLOCK, nheads),
        log_decay.reshape(blocks, BLOCK, nheads),
        b_in.reshape(blocks, BLOCK, -1),
        c_in.reshape(blocks, BLOCK, -1),
    )

    def advance(state, block):
        x_blk, dt_blk, ld_blk, b_blk, c_blk = block
        cumul = jnp.cumsum(ld_blk, axis=0)
        tail = cumul[-1]
        inflow = jnp.exp(tail[None] - cumul) * dt_blk
        fresh = state * jnp.exp(tail)[:, None, None] + jnp.einsum(
            "sh,shp,sn->hpn", inflow, x_blk, b_blk, precision=HIGH
        )
        if not with_out:
            return (fresh, None)
        scores = jnp.dot(c_blk, b_blk.T, precision=HIGH)
        gaps = cumul.T[:, :, None] - cumul.T[:, None, :]
        weights = jnp.exp(jnp.where(lower[None], gaps, -1e30)) * scores[None] * dt_blk.T[:, None, :]
        y_blk = jnp.einsum("hts,shp->thp", weights, x_blk, precision=HIGH)
        y_blk = (
            y_blk
            + jnp.einsum("tn,hpn->thp", c_blk, state, precision=HIGH) * jnp.exp(cumul)[:, :, None]
        )
        y_blk = y_blk + d_skip[None, :, None] * x_blk
        return (fresh, y_blk)

    final, outs = lax.scan(advance, s_init, parts)
    return (outs, final)


def mixer(zx_f, dtr_f, bc_f, dt_bias, a_log, d_skip, s_init):
    z_gate, x_in, dt_val, log_decay, b_in, c_in = split_inputs(zx_f, dtr_f, bc_f, dt_bias, a_log)
    outs, final = ssd_pass(x_in, dt_val, log_decay, b_in, c_in, d_skip, s_init, True)
    return outs.reshape(z_gate.shape[0], -1) * jax.nn.silu(z_gate)


def local_states(zx_f, dtr_f, bc_f, dt_bias, a_log):
    z_gate, x_in, dt_val, log_decay, b_in, c_in = split_inputs(zx_f, dtr_f, bc_f, dt_bias, a_log)
    start_state = jnp.zeros((x_in.shape[1], x_in.shape[2], b_in.shape[1]), x_in.dtype)
    outs, final = ssd_pass(x_in, dt_val, log_decay, b_in, c_in, None, start_state, False)
    return (final, jnp.sum(log_decay, axis=0))


def combine(earlier, later):
    return (earlier[0] * later[0], later[0][:, None, None] * earlier[1] + later[1])


def to_columns(tile):
    n_seq, n_head = (lax.axis_size("seq"), lax.axis_size("head"))
    if n_seq == n_head:
        pairs = [(s * n_head + h, h * n_head + s) for s in range(n_seq) for h in range(n_head)]
        moved = lax.ppermute(tile, ("seq", "head"), pairs)
        return lax.all_gather(moved, "head", axis=0, tiled=True)
    rows = lax.all_gather(tile, "head", axis=1, tiled=True)
    return lax.all_to_all(rows, "seq", split_axis=1, concat_axis=0, tiled=True)


def from_columns(partial_value):
    n_seq, n_head = (lax.axis_size("seq"), lax.axis_size("head"))
    if n_seq == n_head:
        summed = lax.psum_scatter(partial_value, "head", scatter_dimension=0, tiled=True)
        pairs = [(s * n_head + h, h * n_head + s) for s in range(n_seq) for h in range(n_head)]
        return lax.ppermute(summed, ("seq", "head"), pairs)
    rows = lax.all_to_all(partial_value, "seq", split_axis=0, concat_axis=1, tiled=True)
    return lax.psum_scatter(rows, "head", scatter_dimension=1, tiled=True)


def on_device(hidden, w_zx, w_dt, w_bc, dt_bias, a_log, d_skip, norm_gain, w_out, grad_out):
    f32, bf16 = (jnp.float32, jnp.bfloat16)
    tokens = hidden.shape[0]
    wide = HEADS * HDIM
    rows_here = w_zx.shape[0]
    local_cols = w_zx.shape[1] * w_zx.shape[2]
    bc_cols = w_bc.shape[1] * w_bc.shape[2]
    head_cols = w_dt.shape[1]
    w_zx2 = w_zx.reshape(rows_here, local_cols)
    w_bc2 = w_bc.reshape(rows_here, bc_cols)
    hid = to_columns(hidden)
    gout = to_columns(grad_out)

    def summed(partial_value):
        return lax.psum_scatter(partial_value.astype(bf16), "seq", scatter_dimension=0, tiled=True)

    bc_b = summed(jnp.dot(hid, w_bc2, preferred_element_type=f32))
    dtr_b = lax.psum_scatter(
        jnp.dot(hid, w_dt, preferred_element_type=f32), "seq", scatter_dimension=0, tiled=True
    )
    zx_b = summed(jnp.dot(hid, w_zx2, preferred_element_type=f32))
    grad_gated = summed(jnp.einsum("td,kd->tk", gout, w_out, preferred_element_type=f32))
    zx_f = zx_b.astype(f32).reshape(tokens, 2, -1)
    dtr_f = dtr_b.astype(f32)
    bc_f = bc_b.astype(f32).reshape(tokens, 2, -1)
    (s_local, log_total), pull_states = jax.vjp(local_states, zx_f, dtr_f, bc_f, dt_bias, a_log)
    decay = jnp.exp(log_total)
    identity = (jnp.ones_like(decay), jnp.zeros_like(s_local))
    s_in = entering((decay, s_local), "seq", combine, identity)[1]
    mixed, pull_mixer = jax.vjp(mixer, zx_f, dtr_f, bc_f, dt_bias, a_log, d_skip, s_in)
    squares = lax.psum(jnp.sum(mixed * mixed, axis=1), "head")
    rinv = lax.rsqrt(squares / wide + EPS_NORM)
    gated = (mixed * rinv[:, None] * norm_gain[None]).astype(bf16)
    gated_all = lax.all_gather(gated, "seq", axis=0, tiled=True)
    layer_out = from_columns(jnp.dot(gated_all, w_out, preferred_element_type=f32).astype(bf16))
    grad_wout = jnp.einsum("tk,td->kd", gated_all, gout, preferred_element_type=f32)
    upstream = grad_gated.astype(f32)
    gain_part = jnp.sum(upstream * mixed * rinv[:, None], axis=0)
    inner = lax.psum(jnp.sum(upstream * norm_gain[None] * mixed, axis=1), "head")
    grad_mixed = (
        rinv[:, None] * norm_gain[None] * upstream
        - mixed * (rinv * rinv * rinv * inner / wide)[:, None]
    )
    first = pull_mixer(grad_mixed)
    ds_in = first[6]
    carried = carried_in((decay, ds_in), "seq", combine, identity)[1]
    grad_log = decay * jnp.sum(carried * s_in, axis=(1, 2))
    second = pull_states((carried, grad_log))
    d_zx = (first[0] + second[0]).reshape(tokens, -1).astype(bf16)
    d_dtr = (first[1] + second[1]).astype(bf16)
    d_bc = (first[2] + second[2]).reshape(tokens, -1)
    grad_dtbias, grad_alog, grad_dskip, grad_gain = lax.psum(
        (first[3] + second[3], first[4] + second[4], first[5], gain_part), "seq"
    )
    bc_total = lax.psum(d_bc, "head").astype(bf16)
    bc_all = lax.all_gather(bc_total, "seq", axis=0, tiled=True)
    dt_all = lax.all_gather(d_dtr, "seq", axis=0, tiled=True)
    zx_all = lax.all_gather(d_zx, "seq", axis=0, tiled=True)
    share = jnp.arange(bc_cols) * lax.axis_size("head") // bc_cols == lax.axis_index("head")
    term = jnp.einsum("tc,dc->td", zx_all, w_zx2, preferred_element_type=f32)
    term = term + jnp.einsum("th,dh->td", dt_all, w_dt, preferred_element_type=f32)
    term = term + jnp.einsum(
        "tc,dc->td", jnp.where(share[None], bc_all, 0), w_bc2, preferred_element_type=f32
    )
    grad_hidden = from_columns(term.astype(bf16))
    grad_wzx = jnp.einsum("tr,tc->rc", hid, zx_all, preferred_element_type=f32)
    grad_wdt = jnp.einsum("tr,th->rh", hid, dt_all, preferred_element_type=f32)
    grad_wbc = jnp.einsum("tr,tc->rc", hid, bc_all, preferred_element_type=f32)
    return (
        layer_out,
        grad_hidden,
        grad_wzx.reshape(rows_here, 2, -1),
        grad_wdt,
        grad_wbc.reshape(rows_here, 2, -1),
        grad_dtbias,
        grad_alog,
        grad_dskip,
        grad_gain,
        grad_wout,
    )


def solution(mesh):
    in_specs = (
        P(("groups", "seq"), "head"),
        P("seq", None, "head"),
        P("seq", "head"),
        P("seq", None, None),
        P("head"),
        P("head"),
        P("head"),
        P("head"),
        P("head", "seq"),
        P(("groups", "seq"), "head"),
    )
    out_specs = (
        P(("groups", "seq"), "head"),
        P(("groups", "seq"), "head"),
        P(("groups", "seq"), None, "head"),
        P(("groups", "seq"), "head"),
        P(("groups", "seq"), None, None),
        P(("groups", "head")),
        P(("groups", "head")),
        P(("groups", "head")),
        P(("groups", "head")),
        P(("groups", "head"), "seq"),
    )
    return jax.shard_map(
        on_device, mesh=mesh, in_specs=in_specs, out_specs=out_specs, check_vma=False
    )
```

```python
import functools

import jax
import jax.numpy as jnp
from jax import lax
from jax.experimental import pallas as pl
from jax.experimental.pallas import tpu as pltpu
from jax.sharding import PartitionSpec as P

HEADS = 48
HDIM = 64
LANES = 128
EPS_NORM = 1e-05
HIGH = lax.Precision.HIGHEST
F32 = jnp.float32
BF16 = jnp.bfloat16
EXTRA = 16


def mm(a, b, contract=(1, 0), precision=None):
    return lax.dot_general(
        a,
        b,
        (((contract[0],), (contract[1],)), ((), ())),
        preferred_element_type=F32,
        precision=precision,
    )


def iota(shape, dim):
    return lax.broadcasted_iota(jnp.int32, shape, dim)


def spread_matrix(width):
    return (iota((LANES, width), 1) // HDIM == iota((LANES, width), 0)).astype(F32)


def spread(per_head, width):
    return mm(per_head, spread_matrix(width), precision=HIGH)


def gather_heads(values):
    return mm(values, spread_matrix(values.shape[1]), (1, 1), precision=HIGH)


def step_sizes(dtr, dt_bias, a_log):
    rows = dtr.shape[0]
    dt_val = jax.nn.softplus(dtr.astype(F32) + dt_bias)
    log_decay = -dt_val * jnp.exp(a_log)
    lower = (iota((rows, rows), 0) >= iota((rows, rows), 1)).astype(F32)
    return (dt_val, log_decay, mm(lower, log_decay, precision=HIGH))


def state_column(row, width):
    pick = iota((width, LANES), 0) // HDIM == iota((width, LANES), 1)
    return jnp.sum(jnp.where(pick, row, 0.0), axis=1, keepdims=True)


def half_masks(rows):
    low = iota((rows, LANES), 1) < HDIM
    return (low, jnp.logical_not(low))


def states_kernel(xr_ref, bcdt_ref, bias_ref, alog_ref, out_ref):
    rows, width = xr_ref.shape
    n_state = (bcdt_ref.shape[1] - LANES) // 2
    dt_val, _, cumul = step_sizes(bcdt_ref[:, 2 * n_state :], bias_ref[...], alog_ref[...])
    tail = cumul[rows - 1 : rows, :]
    x_in = jax.nn.silu(xr_ref[...].astype(F32))
    inflow = (spread(jnp.exp(tail - cumul) * dt_val, width) * x_in).astype(BF16)
    state = mm(inflow, bcdt_ref[:, :n_state], (0, 0))
    out_ref[:width, :] = state.astype(BF16)
    decay = jnp.exp(tail)
    upper = decay.astype(BF16)
    rest = (decay - upper.astype(F32)).astype(BF16)
    at = iota((EXTRA, LANES), 0)
    out_ref[width:, :] = jnp.where(
        at == 0, upper.astype(F32), jnp.where(at == 1, rest.astype(F32), 0.0)
    ).astype(BF16)


def within_kernel(xr_ref, bcdt_ref, bias_ref, alog_ref, skip_ref, y_ref):
    rows, width = xr_ref.shape
    n_state = (bcdt_ref.shape[1] - LANES) // 2
    dt_val, _, cumul = step_sizes(bcdt_ref[:, 2 * n_state :], bias_ref[...], alog_ref[...])
    x_in = jax.nn.silu(xr_ref[...].astype(F32))
    x_dt = (spread(dt_val, width) * x_in).astype(BF16)
    scores = mm(bcdt_ref[:, n_state : 2 * n_state], bcdt_ref[:, :n_state], (1, 1))
    seen = iota((rows, rows), 0) >= iota((rows, rows), 1)
    across = jnp.transpose(cumul)
    halves = half_masks(rows)
    for pair in range(width // LANES):
        cols = slice(pair * LANES, (pair + 1) * LANES)
        total = skip_ref[:, cols] * x_in[:, cols]
        for side in range(2):
            head = 2 * pair + side
            gaps = cumul[:, head : head + 1] - across[head : head + 1, :]
            weights = (jnp.exp(jnp.where(seen, gaps, -1e30)) * scores).astype(BF16)
            total = total + mm(weights, jnp.where(halves[side], x_dt[:, cols], 0))
        y_ref[:, cols] = total


def fold(from_far, width):
    state = jnp.zeros((width, LANES), F32)
    for part in from_far:
        decay = state_column(
            part[width : width + 1, :].astype(F32) + part[width + 1 : width + 2, :].astype(F32), width
        )
        state = decay * state + part[:width, :].astype(F32)
    return state


def mixed_kernel(*refs):
    parts = refs[:-10]
    y_ref, z_ref, bcdt_ref, bias_ref, alog_ref, gain_ref, gg_ref, s_ref, out_ref, sums_ref = refs[-10:]
    rows, width = y_ref.shape
    n_state = (bcdt_ref.shape[1] - LANES) // 2
    _, _, cumul = step_sizes(bcdt_ref[:, 2 * n_state :], bias_ref[...], alog_ref[...])
    state = fold([part[...] for part in parts], width)
    s_ref[...] = state
    flow = mm(bcdt_ref[:, n_state : 2 * n_state], state.astype(BF16), (1, 1))
    y_val = y_ref[...] + flow * jnp.exp(spread(cumul, width))
    out_ref[...] = y_val
    mixed = y_val * jax.nn.silu(z_ref[...].astype(F32))
    squares = jnp.sum(mixed * mixed, axis=1, keepdims=True)
    inner = jnp.sum(gg_ref[...].astype(F32) * gain_ref[...] * mixed, axis=1, keepdims=True)
    at = iota((rows, LANES), 1)
    sums = jnp.where(at == 0, squares, jnp.where(at == 1, inner, 0.0))
    sums_ref[...] = jnp.transpose(sums)[:8]


def norm_kernel(
    sums_ref, y_ref, z_ref, bcdt_ref, bias_ref, alog_ref, gain_ref, gg_ref, decay_ref,
    gated_ref, dz_ref, gy_ref, ds_ref, gg_out_ref, *, wide
):
    rows, width = y_ref.shape
    n_state = (bcdt_ref.shape[1] - LANES) // 2
    _, _, cumul = step_sizes(bcdt_ref[:, 2 * n_state :], bias_ref[...], alog_ref[...])
    sums = jnp.transpose(sums_ref[...])
    rinv = lax.rsqrt(sums[:, 0:1] / wide + EPS_NORM)
    inner = sums[:, 1:2]
    z_val = z_ref[...].astype(F32)
    sig = jax.nn.sigmoid(z_val)
    gate = z_val * sig
    y_val = y_ref[...]
    mixed = y_val * gate
    upstream = gg_ref[...].astype(F32)
    gain = gain_ref[...]
    normed = mixed * rinv
    gated_ref[...] = (normed * gain).astype(BF16)
    gg_out_ref[...] = jnp.sum(upstream * normed, axis=0, keepdims=True)
    grad_mixed = rinv * gain * upstream - mixed * (rinv * rinv * rinv * inner / wide)
    dz_ref[...] = (grad_mixed * y_val * (sig * (1.0 + z_val * (1.0 - sig)))).astype(BF16)
    grad_y = grad_mixed * gate
    gy_ref[...] = grad_y
    flow = (grad_y * jnp.exp(spread(cumul, width))).astype(BF16)
    ds_ref[:width, :] = mm(flow, bcdt_ref[:, n_state : 2 * n_state], (0, 0)).astype(BF16)
    ds_ref[width:, :] = decay_ref[...]


def back_within_kernel(
    xr_ref, bcdt_ref, bias_ref, alog_ref, gy_ref, dx_ref, dbc_ref
):
    rows, width = xr_ref.shape
    n_state = (bcdt_ref.shape[1] - LANES) // 2
    dt_val, _, cumul = step_sizes(bcdt_ref[:, 2 * n_state :], bias_ref[...], alog_ref[...])
    x_in = jax.nn.silu(xr_ref[...].astype(F32))
    x_dt = (spread(dt_val, width) * x_in).astype(BF16)
    grad_y = gy_ref[...].astype(BF16)
    b_in = bcdt_ref[:, :n_state]
    c_in = bcdt_ref[:, n_state : 2 * n_state]
    scores = mm(b_in, c_in, (1, 1))
    seen = iota((rows, rows), 1) >= iota((rows, rows), 0)
    across = jnp.transpose(cumul)
    halves = half_masks(rows)
    d_scores = jnp.zeros((rows, rows), F32)
    for pair in range(width // LANES):
        cols = slice(pair * LANES, (pair + 1) * LANES)
        total = jnp.zeros((rows, LANES), F32)
        for side in range(2):
            head = 2 * pair + side
            gaps = across[head : head + 1, :] - cumul[:, head : head + 1]
            fade = jnp.exp(jnp.where(seen, gaps, -1e30))
            total = total + mm(
                (fade * scores).astype(BF16), jnp.where(halves[side], grad_y[:, cols], 0)
            )
            d_scores = d_scores + fade * mm(
                jnp.where(halves[side], x_dt[:, cols], 0), grad_y[:, cols], (1, 1)
            )
        dx_ref[:, cols] = total
    d_scores = d_scores.astype(BF16)
    dbc_ref[:, :n_state] = mm(d_scores, c_in)
    dbc_ref[:, n_state:] = mm(d_scores, b_in, (0, 0))


def back_kernel(*refs):
    parts = refs[:-14]
    s_ref, xr_ref, bcdt_ref, bias_ref, alog_ref, skip_ref, y_ref, gy_ref, dxw_ref, dbcw_ref = refs[-14:-4]
    dx_ref, dbc_ref, small_ref, dskip_ref = refs[-4:]
    rows, width = xr_ref.shape
    n_state = (bcdt_ref.shape[1] - LANES) // 2
    dtr = bcdt_ref[:, 2 * n_state :].astype(F32)
    dt_val, log_decay, cumul = step_sizes(dtr, bias_ref[...], alog_ref[...])
    tail = cumul[rows - 1 : rows, :]
    b_in = bcdt_ref[:, :n_state]
    state = s_ref[...]
    later = fold([part[...] for part in parts], width)
    later_b = later.astype(BF16)
    raw = xr_ref[...].astype(F32)
    sig = jax.nn.sigmoid(raw)
    x_in = raw * sig
    cum_wide = spread(cumul, width)
    fade_out = jnp.exp(cum_wide[rows - 1 : rows, :] - cum_wide)
    dt_wide = spread(dt_val, width)
    grad_y = gy_ref[...]
    skip = skip_ref[...]
    flow = fade_out * mm(b_in, later_b, (1, 1))
    d_xdt = dxw_ref[...] + flow
    x_dt = dt_wide * x_in
    d_x = dt_wide * d_xdt + skip * grad_y
    dx_ref[...] = (d_x * (sig * (1.0 + raw * (1.0 - sig)))).astype(BF16)
    d_dt = gather_heads(x_in * d_xdt)
    moved = gather_heads(grad_y * (y_ref[...] - skip * x_in)) - dt_val * d_dt
    tail_part = jnp.sum(gather_heads(x_dt * flow), axis=0, keepdims=True)
    pairs = jnp.sum(later * state, axis=1, keepdims=True)
    pick = iota((width, LANES), 0) // HDIM == iota((width, LANES), 1)
    state_part = jnp.sum(jnp.where(pick, pairs, 0.0), axis=0, keepdims=True) * jnp.exp(tail)
    upper = (iota((rows, rows), 1) >= iota((rows, rows), 0)).astype(F32)
    d_log = mm(upper, moved, precision=HIGH) + tail_part + state_part
    d_dt = d_dt - jnp.exp(alog_ref[...]) * d_log
    d_dtr = d_dt * jax.nn.sigmoid(dtr + bias_ref[...])
    at = iota((8, LANES), 0)
    d_bias = jnp.sum(d_dtr, axis=0, keepdims=True)
    d_alog = jnp.sum(d_log * log_decay, axis=0, keepdims=True)
    small_ref[...] = jnp.where(at == 0, d_bias, jnp.where(at == 1, d_alog, 0.0))
    dskip_ref[...] = jnp.sum(grad_y * x_in, axis=0, keepdims=True)
    inflow = (fade_out * x_dt).astype(BF16)
    dbc_ref[:, :n_state] = (dbcw_ref[:, :n_state] + mm(inflow, later_b)).astype(BF16)
    outflow = (grad_y * jnp.exp(cum_wide)).astype(BF16)
    dbc_ref[:, n_state : 2 * n_state] = (
        dbcw_ref[:, n_state:] + mm(outflow, state.astype(BF16))
    ).astype(BF16)
    dbc_ref[:, 2 * n_state :] = d_dtr.astype(BF16)


def call(kernel, *outs):
    def run(*args):
        vmem = pl.BlockSpec(memory_space=pltpu.VMEM)
        return pl.pallas_call(
            kernel,
            out_shape=[jax.ShapeDtypeStruct(*o) for o in outs],
            in_specs=[vmem] * len(args),
            out_specs=[vmem] * len(outs),
            compiler_params=pltpu.CompilerParams(vmem_limit_bytes=48 * 1024 * 1024),
        )(*args)

    return run


def square():
    return lax.axis_size("seq") == 4 and lax.axis_size("head") == 4


def exchange(tile, bit):
    return lax.ppermute(tile, "head", [(h, h ^ bit) for h in range(lax.axis_size("head"))])


def head_gather(tile):
    me = lax.axis_index("head")
    chip, core = (me // 2, me % 2)
    other = exchange(tile, 2)
    mine = jnp.stack([jnp.where(chip == 0, tile, other), jnp.where(chip == 0, other, tile)])
    across = exchange(mine, 1)
    first, second = (jnp.where(core == 0, mine, across), jnp.where(core == 0, across, mine))
    return jnp.stack([first[0], second[0], first[1], second[1]])


def head_sum(parts):
    me = lax.axis_index("head")
    chip, core = (me // 2, me % 2)
    even, odd = (parts[0::2], parts[1::2])
    got = exchange(jnp.where(core == 0, odd, even), 1)
    half = (jnp.where(core == 0, even, odd).astype(F32) + got.astype(F32)).astype(BF16)
    got = exchange(jnp.where(chip == 0, half[1], half[0]), 2)
    return (jnp.where(chip == 0, half[0], half[1]).astype(F32) + got.astype(F32)).astype(BF16)


def transposed(tile):
    n_seq, n_head = (lax.axis_size("seq"), lax.axis_size("head"))
    pairs = [(s * n_head + h, h * n_head + s) for s in range(n_seq) for h in range(n_head)]
    return lax.ppermute(tile, ("seq", "head"), pairs)


def to_columns(tile):
    if square():
        stacked = head_gather(transposed(tile))
        return stacked.reshape(-1, stacked.shape[-1])
    rows = lax.all_gather(tile, "head", axis=1, tiled=True)
    return lax.all_to_all(rows, "seq", split_axis=1, concat_axis=0, tiled=True)


def from_columns(partial_value):
    if square():
        return transposed(head_sum(partial_value.reshape(4, -1, partial_value.shape[-1])))
    rows = lax.all_to_all(partial_value, "seq", split_axis=0, concat_axis=1, tiled=True)
    return lax.psum_scatter(rows, "head", scatter_dimension=1, tiled=True)


def feature_blocks(tile):
    if square():
        return list(head_gather(tile))
    return jnp.split(lax.all_gather(tile, "head", axis=1, tiled=True), lax.axis_size("seq"), axis=1)


def sum_blocks(blocks):
    if square():
        return head_sum(jnp.stack(blocks))
    return lax.psum_scatter(jnp.concatenate(blocks, axis=1), "head", scatter_dimension=1, tiled=True)


def shards_before(packed, step):
    n_seq = lax.axis_size("seq")
    if n_seq <= 4:
        return [
            lax.ppermute(
                packed, "seq", [(s, s + k * step) for s in range(n_seq) if 0 <= s + k * step < n_seq]
            )
            for k in range(n_seq - 1, 0, -1)
        ]
    everything = lax.all_gather(packed, "seq")
    here = lax.axis_index("seq")
    parts = []
    for k in range(n_seq - 1, 0, -1):
        at = here - k * step
        part = lax.dynamic_index_in_dim(everything, jnp.clip(at, 0, n_seq - 1), 0, keepdims=False)
        parts.append(jnp.where((at >= 0) & (at < n_seq), part, 0))
    return parts


def all_output_weights(w_out):
    groups = lax.axis_size("groups")
    if groups != 2:
        return lax.all_gather(w_out, "seq")
    me = lax.axis_index("groups")
    half = w_out.shape[0] // 2
    part = lax.dynamic_slice_in_dim(w_out, me * half, half, 0)
    mine = lax.all_gather(part, "seq")
    other = lax.ppermute(mine, "groups", [(0, 1), (1, 0)])
    return jnp.concatenate(
        [jnp.where(me == 0, mine, other), jnp.where(me == 0, other, mine)], axis=1
    )


def seq_blocks(value):
    n_seq = lax.axis_size("seq")
    if n_seq > 4:
        return list(enumerate(lax.all_gather(value, "seq")))
    here = lax.axis_index("seq")
    shards = [(here, value)]
    for k in range(1, n_seq):
        moved = lax.ppermute(value, "seq", [(s, (s + k) % n_seq) for s in range(n_seq)])
        shards.append(((here - k) % n_seq, moved))
    return shards


def seq_stack(value):
    n_seq = lax.axis_size("seq")
    shards = seq_blocks(value)
    if n_seq > 4:
        return jnp.concatenate([part for _, part in shards])
    stacked = jnp.stack([part for _, part in shards])
    here = lax.axis_index("seq")
    return jnp.concatenate(
        [
            lax.dynamic_index_in_dim(stacked, (here - j) % n_seq, 0, keepdims=False)
            for j in range(n_seq)
        ]
    )


def summed_rows(partial_value):
    return lax.psum_scatter(partial_value.astype(BF16), "seq", scatter_dimension=0, tiled=True)


def all_rows(value):
    return lax.all_gather(value, "seq", axis=0, tiled=True)


def tie(value, *after):
    return lax.optimization_barrier((value, *after))[0]


def on_device(hidden, w_zx, w_dt, w_bc, dt_bias, a_log, d_skip, norm_gain, w_out, grad_out):
    rows = hidden.shape[0]
    wide = HEADS * HDIM
    rows_here = w_zx.shape[0]
    width = w_zx.shape[2]
    bc_cols = w_bc.shape[1] * w_bc.shape[2]
    nheads = w_dt.shape[1]
    n_head = lax.axis_size("head")
    quarter = bc_cols // n_head
    w_z = w_zx[:, 0]
    w_x = w_zx[:, 1]
    w_bcq = lax.dynamic_slice_in_dim(
        w_bc.reshape(rows_here, bc_cols), lax.axis_index("head") * quarter, quarter, 1
    )
    w_small = jnp.concatenate(
        [w_bcq, w_dt, jnp.zeros((rows_here, LANES - quarter - nheads), BF16)], axis=1
    )
    pad = ((0, 0), (0, LANES - nheads))
    bias = jnp.pad(dt_bias[None], pad)
    alog = jnp.pad(a_log[None], pad)
    skip = jnp.repeat(d_skip, HDIM)[None]
    gain = norm_gain[None]

    if square():
        moved = transposed(hidden)
        hid = head_gather(moved)
        hid = hid.reshape(-1, hid.shape[-1])
    else:
        hid = moved = to_columns(hidden)
    part_x = mm(hid, w_x).astype(BF16)
    hid_z, part_x = lax.optimization_barrier((hid, part_x))
    xr = summed_rows(part_x)
    part_z = mm(hid_z, w_z).astype(BF16)
    zr = summed_rows(part_z)
    w_full = all_output_weights(w_out)

    row_blocks = feature_blocks(tie(hidden, moved))
    small_t = jnp.transpose(w_small)[: (quarter + nheads + 15) // 16 * 16]
    shards = seq_blocks(tie(small_t, moved))
    row_stack = jnp.stack(row_blocks)
    small = sum(
        mm(lax.dynamic_index_in_dim(row_stack, at, 0, keepdims=False), part, (1, 1))
        for at, part in shards
    )
    small = jnp.pad(small.astype(BF16), ((0, 0), (0, LANES - small.shape[1])))
    pieces = head_gather(small) if square() else lax.all_gather(small, "head")
    bcdt = jnp.concatenate(
        [pieces[k, :, :quarter] for k in range(n_head)]
        + [jnp.pad(small[:, quarter : quarter + nheads], pad)],
        axis=1,
    )
    gout_blocks = feature_blocks(tie(grad_out, part_x))
    grad_gated = sum(mm(g, w_full[i], (1, 1)) for i, g in enumerate(gout_blocks)).astype(BF16)
    gout = to_columns(tie(grad_out, part_z))

    packed = ((width + EXTRA, LANES), BF16)
    flat = (rows, width)
    (local,) = call(states_kernel, packed)(xr, bcdt, bias, alog)
    before = shards_before(local, 1)
    (y_own,) = call(within_kernel, (flat, F32))(xr, bcdt, bias, alog, skip)
    s_in, y_val, sums = call(mixed_kernel, ((width, LANES), F32), (flat, F32), ((8, rows), F32))(
        *before, y_own, zr, bcdt, bias, alog, gain, grad_gated
    )
    sums = lax.psum(sums, "head")
    gated, d_z, grad_y, d_state, gain_part = call(
        functools.partial(norm_kernel, wide=wide),
        (flat, BF16),
        (flat, BF16),
        (flat, F32),
        packed,
        ((1, width), F32),
    )(sums, y_val, zr, bcdt, bias, alog, gain, grad_gated, local[width:])
    later = shards_before(d_state, -1)
    dx_own, dbc_own = call(back_within_kernel, (flat, F32), ((rows, bc_cols), F32))(
        xr, bcdt, bias, alog, grad_y
    )
    d_x, d_bcdt, sums_small, dskip_part = call(
        back_kernel,
        (flat, BF16),
        ((rows, bc_cols + LANES), BF16),
        ((8, LANES), F32),
        ((1, width), F32),
    )(*later, s_in, xr, bcdt, bias, alog, skip, y_val, grad_y, dx_own, dbc_own)

    dz_all = all_rows(d_z)
    dx_all = all_rows(d_x)
    quarters = [d_bcdt[:, k * quarter : (k + 1) * quarter] for k in range(n_head)]
    if square():
        d_bcq = head_sum(jnp.stack(quarters))
    else:
        d_bcq = lax.psum_scatter(jnp.stack(quarters), "head", scatter_dimension=0)
    d_small = jnp.concatenate(
        [
            d_bcq,
            d_bcdt[:, bc_cols : bc_cols + nheads],
            jnp.zeros((rows, LANES - quarter - nheads), BF16),
        ],
        axis=1,
    )
    small_all = seq_stack(d_small)
    layer_blocks = [mm(gated, w_full[i]).astype(BF16) for i in range(len(gout_blocks))]
    layer_out = sum_blocks(layer_blocks)
    param_sums = lax.psum(
        (
            sums_small[0, :nheads],
            sums_small[1, :nheads],
            jnp.sum(dskip_part.reshape(nheads, HDIM), axis=1),
            gain_part[0],
        ),
        "seq",
    )
    grad_wz = mm(hid, dz_all, (0, 0))
    term_z = mm(dz_all, w_z, (1, 1)) + mm(small_all, w_small, (1, 1))
    grad_small = mm(hid, small_all, (0, 0))
    dx_all, param_sums, gated, grad_wz, grad_small, term_z, gout = lax.optimization_barrier(
        (dx_all, param_sums, gated, grad_wz, grad_small, term_z, gout)
    )
    gated_all = all_rows(gated)
    term = (term_z + mm(dx_all, w_x, (1, 1))).astype(BF16)
    grad_hidden = from_columns(term)
    grad_wx = mm(tie(hid, term), dx_all, (0, 0))
    grad_wbcq = grad_small[:, :quarter].astype(BF16)
    grad_wbc = head_gather(grad_wbcq) if square() else lax.all_gather(grad_wbcq, "head")
    grad_wbc = jnp.concatenate(list(grad_wbc), axis=1).astype(F32)
    grad_wzx = jnp.stack([grad_wz, grad_wx], axis=1)
    grad_wout = mm(gated_all, gout, (0, 0))
    grad_dtbias, grad_alog, grad_dskip, grad_gain = param_sums
    return (
        layer_out,
        grad_hidden,
        grad_wzx,
        grad_small[:, quarter : quarter + nheads],
        grad_wbc.reshape(w_bc.shape),
        grad_dtbias,
        grad_alog,
        grad_dskip,
        grad_gain,
        grad_wout,
    )


def solution(mesh):
    in_specs = (
        P(("groups", "seq"), "head"),
        P("seq", None, "head"),
        P("seq", "head"),
        P("seq", None, None),
        P("head"),
        P("head"),
        P("head"),
        P("head"),
        P("head", "seq"),
        P(("groups", "seq"), "head"),
    )
    out_specs = (
        P(("groups", "seq"), "head"),
        P(("groups", "seq"), "head"),
        P(("groups", "seq"), None, "head"),
        P(("groups", "seq"), "head"),
        P(("groups", "seq"), None, None),
        P(("groups", "head")),
        P(("groups", "head")),
        P(("groups", "head")),
        P(("groups", "head")),
        P(("groups", "head"), "seq"),
    )
    return jax.shard_map(
        on_device, mesh=mesh, in_specs=in_specs, out_specs=out_specs, check_vma=False
    )
```

```python
import functools

import jax
import jax.numpy as jnp
from jax import lax
from jax.experimental import pallas as pl
from jax.experimental.pallas import tpu as pltpu
from jax.sharding import PartitionSpec as P

HEADS = 48
HDIM = 64
LANES = 128
EPS_NORM = 1e-05
HIGH = lax.Precision.HIGHEST
F32 = jnp.float32
BF16 = jnp.bfloat16
EXTRA = 16


def mm(a, b, contract=(1, 0), precision=None):
    return lax.dot_general(
        a,
        b,
        (((contract[0],), (contract[1],)), ((), ())),
        preferred_element_type=F32,
        precision=precision,
    )


def iota(shape, dim):
    return lax.broadcasted_iota(jnp.int32, shape, dim)


def spread_matrix(width):
    return (iota((LANES, width), 1) // HDIM == iota((LANES, width), 0)).astype(F32)


def spread(per_head, width):
    return mm(per_head, spread_matrix(width), precision=HIGH)


def gather_heads(values):
    return mm(values, spread_matrix(values.shape[1]), (1, 1), precision=HIGH)


def step_sizes(dtr, dt_bias, a_log):
    rows = dtr.shape[0]
    dt_val = jax.nn.softplus(dtr.astype(F32) + dt_bias)
    log_decay = -dt_val * jnp.exp(a_log)
    lower = (iota((rows, rows), 0) >= iota((rows, rows), 1)).astype(F32)
    return (dt_val, log_decay, mm(lower, log_decay, precision=HIGH))


def state_column(row, width):
    pick = iota((width, LANES), 0) // HDIM == iota((width, LANES), 1)
    return jnp.sum(jnp.where(pick, row, 0.0), axis=1, keepdims=True)


def half_masks(rows):
    low = iota((rows, LANES), 1) < HDIM
    return (low, jnp.logical_not(low))


def steps_kernel(bcdt_ref, bias_ref, alog_ref, dt_ref, cum_ref, dtw_ref, cumw_ref):
    width = dtw_ref.shape[1]
    dt_val, _, cumul = step_sizes(
        bcdt_ref[:, bcdt_ref.shape[1] - LANES :], bias_ref[...], alog_ref[...]
    )
    dt_ref[...] = dt_val
    cum_ref[...] = cumul
    dtw_ref[...] = spread(dt_val, width)
    cumw_ref[...] = spread(cumul, width)


def states_kernel(xr_ref, bcdt_ref, cum_ref, dtw_ref, cumw_ref, out_ref):
    rows, width = xr_ref.shape
    n_state = (bcdt_ref.shape[1] - LANES) // 2
    x_in = jax.nn.silu(xr_ref[...].astype(F32))
    cum_wide = cumw_ref[...]
    fade_out = jnp.exp(cum_wide[rows - 1 : rows, :] - cum_wide)
    state = mm((fade_out * dtw_ref[...] * x_in).astype(BF16), bcdt_ref[:, :n_state], (0, 0))
    out_ref[:width, :] = state.astype(BF16)
    decay = jnp.exp(cum_ref[rows - 1 : rows, :])
    upper = decay.astype(BF16)
    rest = (decay - upper.astype(F32)).astype(BF16)
    at = iota((EXTRA, LANES), 0)
    out_ref[width:, :] = jnp.where(
        at == 0, upper.astype(F32), jnp.where(at == 1, rest.astype(F32), 0.0)
    ).astype(BF16)


def within_kernel(xr_ref, bcdt_ref, cum_ref, dtw_ref, skip_ref, y_ref):
    rows, width = xr_ref.shape
    n_state = (bcdt_ref.shape[1] - LANES) // 2
    cumul = cum_ref[...]
    x_in = jax.nn.silu(xr_ref[...].astype(F32))
    x_dt = (dtw_ref[...] * x_in).astype(BF16)
    scores = mm(bcdt_ref[:, n_state : 2 * n_state], bcdt_ref[:, :n_state], (1, 1))
    seen = iota((rows, rows), 0) >= iota((rows, rows), 1)
    across = jnp.transpose(cumul)
    halves = half_masks(rows)
    for pair in range(width // LANES):
        cols = slice(pair * LANES, (pair + 1) * LANES)
        total = skip_ref[:, cols] * x_in[:, cols]
        for side in range(2):
            head = 2 * pair + side
            gaps = cumul[:, head : head + 1] - across[head : head + 1, :]
            weights = (jnp.exp(jnp.where(seen, gaps, -1e30)) * scores).astype(BF16)
            total = total + mm(weights, jnp.where(halves[side], x_dt[:, cols], 0))
        y_ref[:, cols] = total


def fold(from_far, width):
    state = from_far[0][:width, :].astype(F32)
    for part in from_far[1:]:
        decay = state_column(
            part[width : width + 1, :].astype(F32) + part[width + 1 : width + 2, :].astype(F32), width
        )
        state = decay * state + part[:width, :].astype(F32)
    return state


def hop_kernel(packed_ref, got_ref, out_ref):
    width = out_ref.shape[0]
    own = packed_ref[:width, :].astype(F32)
    decay = packed_ref[width : width + 1, :].astype(F32) + packed_ref[width + 1 : width + 2, :].astype(F32)
    out_ref[...] = (state_column(decay, width) * got_ref[:width, :].astype(F32) + own).astype(BF16)


def mixed_kernel(*refs):
    parts = refs[:-9]
    y_ref, z_ref, bcdt_ref, cumw_ref, gain_ref, gg_ref, s_ref, out_ref, sums_ref = refs[-9:]
    rows, width = y_ref.shape
    n_state = (bcdt_ref.shape[1] - LANES) // 2
    state = fold([part[...] for part in parts], width)
    s_ref[...] = state
    flow = mm(bcdt_ref[:, n_state : 2 * n_state], state.astype(BF16), (1, 1))
    y_val = y_ref[...] + flow * jnp.exp(cumw_ref[...])
    out_ref[...] = y_val
    mixed = y_val * jax.nn.silu(z_ref[...].astype(F32))
    squares = jnp.sum(mixed * mixed, axis=1, keepdims=True)
    inner = jnp.sum(gg_ref[...].astype(F32) * gain_ref[...] * mixed, axis=1, keepdims=True)
    at = iota((rows, LANES), 1)
    sums = jnp.where(at == 0, squares, jnp.where(at == 1, inner, 0.0))
    sums_ref[...] = jnp.transpose(sums)[:8]


def norm_kernel(
    sums_ref, y_ref, z_ref, bcdt_ref, cumw_ref, gain_ref, gg_ref, decay_ref,
    gated_ref, dz_ref, gy_ref, ds_ref, gg_out_ref, *, wide
):
    rows, width = y_ref.shape
    n_state = (bcdt_ref.shape[1] - LANES) // 2
    sums = jnp.transpose(sums_ref[...])
    rinv = lax.rsqrt(sums[:, 0:1] / wide + EPS_NORM)
    inner = sums[:, 1:2]
    z_val = z_ref[...].astype(F32)
    sig = jax.nn.sigmoid(z_val)
    gate = z_val * sig
    y_val = y_ref[...]
    mixed = y_val * gate
    upstream = gg_ref[...].astype(F32)
    gain = gain_ref[...]
    normed = mixed * rinv
    gated_ref[...] = (normed * gain).astype(BF16)
    gg_out_ref[...] = jnp.sum(upstream * normed, axis=0, keepdims=True)
    grad_mixed = rinv * gain * upstream - mixed * (rinv * rinv * rinv * inner / wide)
    dz_ref[...] = (grad_mixed * y_val * (sig * (1.0 + z_val * (1.0 - sig)))).astype(BF16)
    grad_y = grad_mixed * gate
    gy_ref[...] = grad_y
    flow = (grad_y * jnp.exp(cumw_ref[...])).astype(BF16)
    ds_ref[:width, :] = mm(flow, bcdt_ref[:, n_state : 2 * n_state], (0, 0)).astype(BF16)
    ds_ref[width:, :] = decay_ref[...]


def back_within_kernel(xr_ref, bcdt_ref, cum_ref, dtw_ref, gy_ref, dx_ref, dbc_ref):
    rows, width = xr_ref.shape
    n_state = (bcdt_ref.shape[1] - LANES) // 2
    cumul = cum_ref[...]
    x_in = jax.nn.silu(xr_ref[...].astype(F32))
    x_dt = (dtw_ref[...] * x_in).astype(BF16)
    grad_y = gy_ref[...].astype(BF16)
    b_in = bcdt_ref[:, :n_state]
    c_in = bcdt_ref[:, n_state : 2 * n_state]
    scores = mm(b_in, c_in, (1, 1))
    seen = iota((rows, rows), 1) >= iota((rows, rows), 0)
    across = jnp.transpose(cumul)
    halves = half_masks(rows)
    d_scores = jnp.zeros((rows, rows), F32)
    for pair in range(width // LANES):
        cols = slice(pair * LANES, (pair + 1) * LANES)
        total = jnp.zeros((rows, LANES), F32)
        for side in range(2):
            head = 2 * pair + side
            gaps = across[head : head + 1, :] - cumul[:, head : head + 1]
            fade = jnp.exp(jnp.where(seen, gaps, -1e30))
            total = total + mm(
                (fade * scores).astype(BF16), jnp.where(halves[side], grad_y[:, cols], 0)
            )
            d_scores = d_scores + fade * mm(
                jnp.where(halves[side], x_dt[:, cols], 0), grad_y[:, cols], (1, 1)
            )
        dx_ref[:, cols] = total
    d_scores = d_scores.astype(BF16)
    dbc_ref[:, :n_state] = mm(d_scores, c_in)
    dbc_ref[:, n_state:] = mm(d_scores, b_in, (0, 0))


def back_kernel(*refs):
    parts = refs[:-18]
    s_ref, xr_ref, bcdt_ref, bias_ref, alog_ref, dt_ref, cum_ref, dtw_ref, cumw_ref = refs[-18:-9]
    skip_ref, y_ref, gy_ref, dxw_ref, dbcw_ref = refs[-9:-4]
    dx_ref, dbc_ref, small_ref, dskip_ref = refs[-4:]
    rows, width = xr_ref.shape
    n_state = (bcdt_ref.shape[1] - LANES) // 2
    dtr = bcdt_ref[:, 2 * n_state :].astype(F32)
    dt_val = dt_ref[...]
    rate = jnp.exp(alog_ref[...])
    tail = cum_ref[rows - 1 : rows, :]
    b_in = bcdt_ref[:, :n_state]
    state = s_ref[...]
    later = fold([part[...] for part in parts], width)
    later_b = later.astype(BF16)
    raw = xr_ref[...].astype(F32)
    sig = jax.nn.sigmoid(raw)
    x_in = raw * sig
    cum_wide = cumw_ref[...]
    fade_out = jnp.exp(cum_wide[rows - 1 : rows, :] - cum_wide)
    dt_wide = dtw_ref[...]
    grad_y = gy_ref[...]
    skip = skip_ref[...]
    flow = fade_out * mm(b_in, later_b, (1, 1))
    d_xdt = dxw_ref[...] + flow
    x_dt = (dt_wide * x_in).astype(BF16).astype(F32)
    grad_r = grad_y.astype(BF16).astype(F32)
    d_x = dt_wide * d_xdt + skip * grad_y
    dx_ref[...] = (d_x * (sig * (1.0 + raw * (1.0 - sig)))).astype(BF16)
    d_dt = gather_heads(x_in * d_xdt)
    moved = gather_heads(grad_r * (y_ref[...] - skip * x_in) - x_dt * d_xdt)
    tail_part = jnp.sum(gather_heads(x_dt * flow), axis=0, keepdims=True)
    pairs = jnp.sum(later * state, axis=1, keepdims=True)
    pick = iota((width, LANES), 0) // HDIM == iota((width, LANES), 1)
    state_part = jnp.sum(jnp.where(pick, pairs, 0.0), axis=0, keepdims=True) * jnp.exp(tail)
    upper = (iota((rows, rows), 1) >= iota((rows, rows), 0)).astype(F32)
    d_log = mm(upper, moved, precision=HIGH) + tail_part + state_part
    d_dt = d_dt - rate * d_log
    d_dtr = d_dt * jax.nn.sigmoid(dtr + bias_ref[...])
    at = iota((8, LANES), 0)
    d_bias = jnp.sum(d_dtr, axis=0, keepdims=True)
    d_alog = jnp.sum(d_log * (-dt_val * rate), axis=0, keepdims=True)
    small_ref[...] = jnp.where(at == 0, d_bias, jnp.where(at == 1, d_alog, 0.0))
    dskip_ref[...] = jnp.sum(grad_y * x_in, axis=0, keepdims=True)
    inflow = (fade_out * x_dt).astype(BF16)
    dbc_ref[:, :n_state] = (dbcw_ref[:, :n_state] + mm(inflow, later_b)).astype(BF16)
    outflow = (grad_y * jnp.exp(cum_wide)).astype(BF16)
    dbc_ref[:, n_state : 2 * n_state] = (
        dbcw_ref[:, n_state:] + mm(outflow, state.astype(BF16))
    ).astype(BF16)
    dbc_ref[:, 2 * n_state :] = d_dtr.astype(BF16)


def call(kernel, *outs):
    def run(*args):
        vmem = pl.BlockSpec(memory_space=pltpu.VMEM)
        return pl.pallas_call(
            kernel,
            out_shape=[jax.ShapeDtypeStruct(*o) for o in outs],
            in_specs=[vmem] * len(args),
            out_specs=[vmem] * len(outs),
            compiler_params=pltpu.CompilerParams(vmem_limit_bytes=48 * 1024 * 1024),
        )(*args)

    return run


def square():
    return lax.axis_size("seq") == 4 and lax.axis_size("head") == 4


def exchange(tile, bit):
    return lax.ppermute(tile, "head", [(h, h ^ bit) for h in range(lax.axis_size("head"))])


def lanes():
    me, here = (lax.axis_index("head"), lax.axis_index("seq"))
    return (me // 2, me % 2, here // 2, here % 2)


def head_gather(tile, crossed=False):
    chip, core, high, low = lanes()
    if crossed:
        chip, core = (chip ^ low, core ^ high)
    other = exchange(tile, 2)
    mine = jnp.stack([jnp.where(chip == 0, tile, other), jnp.where(chip == 0, other, tile)])
    across = exchange(mine, 1)
    first, second = (jnp.where(core == 0, mine, across), jnp.where(core == 0, across, mine))
    if crossed:
        return jnp.concatenate([first, second])
    return jnp.stack([first[0], second[0], first[1], second[1]])


def head_sum(parts, crossed=False):
    chip, core, high, low = lanes()
    if crossed:
        chip, core = (chip ^ low, core ^ high)
        zero, one = (parts[:2], parts[2:])
    else:
        zero, one = (parts[0::2], parts[1::2])
    got = exchange(jnp.where(core == 0, one, zero), 1)
    half = (jnp.where(core == 0, zero, one).astype(F32) + got.astype(F32)).astype(BF16)
    got = exchange(jnp.where(chip == 0, half[1], half[0]), 2)
    return (jnp.where(chip == 0, half[0], half[1]).astype(F32) + got.astype(F32)).astype(BF16)


BIT_SWAP = (0, 2, 1, 3)


def transposed(tile):
    out = [(s * 4 + h, s * 4 + BIT_SWAP[s ^ h]) for s in range(4) for h in range(4)]
    over = [(s * 4 + BIT_SWAP[s ^ h], h * 4 + BIT_SWAP[s ^ h]) for s in range(4) for h in range(4)]
    return lax.ppermute(lax.ppermute(tile, ("seq", "head"), out), ("seq", "head"), over)


def transposed_back(tile):
    pairs = [(s * 4 + BIT_SWAP[q ^ s], q * 4 + s) for s in range(4) for q in range(4)]
    return lax.ppermute(tile, ("seq", "head"), pairs)


def to_columns(tile):
    if square():
        stacked = head_gather(transposed(tile), True)
        return stacked.reshape(-1, stacked.shape[-1])
    rows = lax.all_gather(tile, "head", axis=1, tiled=True)
    return lax.all_to_all(rows, "seq", split_axis=1, concat_axis=0, tiled=True)


def from_columns(partial_value):
    if square():
        reduced = head_sum(partial_value.reshape(4, -1, partial_value.shape[-1]), True)
        return (transposed_back(reduced), reduced)
    rows = lax.all_to_all(partial_value, "seq", split_axis=0, concat_axis=1, tiled=True)
    reduced = lax.psum_scatter(rows, "head", scatter_dimension=1, tiled=True)
    return (reduced, reduced)


def feature_blocks(tile):
    if square():
        return list(head_gather(tile))
    return jnp.split(lax.all_gather(tile, "head", axis=1, tiled=True), lax.axis_size("seq"), axis=1)


def sum_blocks(blocks):
    if square():
        return head_sum(blocks)
    return lax.psum_scatter(jnp.concatenate(list(blocks), axis=1), "head", scatter_dimension=1, tiled=True)


def shards_before(packed, step):
    n_seq = lax.axis_size("seq")
    if n_seq == 4:
        width = packed.shape[0] - EXTRA
        near = lax.ppermute(packed, "seq", [(s, s + step) for s in range(4) if 0 <= s + step < 4])
        (both,) = call(hop_kernel, ((width, LANES), BF16))(packed, near)
        far = lax.ppermute(both, "seq", [(s, s + 2 * step) for s in range(4) if 0 <= s + 2 * step < 4])
        return [far, near]
    everything = lax.all_gather(packed, "seq")
    here = lax.axis_index("seq")
    parts = []
    for k in range(n_seq - 1, 0, -1):
        at = here - k * step
        part = lax.dynamic_index_in_dim(everything, jnp.clip(at, 0, n_seq - 1), 0, keepdims=False)
        parts.append(jnp.where((at >= 0) & (at < n_seq), part, 0))
    return parts


def all_output_weights(w_out, after):
    groups = lax.axis_size("groups")
    if groups != 2:
        return lax.all_gather(w_out, "seq")
    me = lax.axis_index("groups")
    half = w_out.shape[0] // 2
    part = lax.dynamic_slice_in_dim(w_out, me * half, half, 0)
    mine = lax.all_gather(part, "seq")
    other = lax.ppermute(tie(mine, after), "groups", [(0, 1), (1, 0)])
    return jnp.concatenate(
        [jnp.where(me == 0, mine, other), jnp.where(me == 0, other, mine)], axis=1
    )


def seq_blocks(value):
    n_seq = lax.axis_size("seq")
    if n_seq > 4:
        return list(enumerate(lax.all_gather(value, "seq")))
    here = lax.axis_index("seq")
    shards = [(here, value)]
    for k in range(1, n_seq):
        moved = lax.ppermute(value, "seq", [(s, (s + k) % n_seq) for s in range(n_seq)])
        shards.append(((here - k) % n_seq, moved))
    return shards


def seq_stack(value):
    n_seq = lax.axis_size("seq")
    shards = seq_blocks(value)
    if n_seq > 4:
        return jnp.concatenate([part for _, part in shards])
    stacked = jnp.stack([part for _, part in shards])
    here = lax.axis_index("seq")
    return jnp.concatenate(
        [
            lax.dynamic_index_in_dim(stacked, (here - j) % n_seq, 0, keepdims=False)
            for j in range(n_seq)
        ]
    )


def summed_rows(partial_value):
    return lax.psum_scatter(partial_value.astype(BF16), "seq", scatter_dimension=0, tiled=True)


def all_rows(value):
    return lax.all_gather(value, "seq", axis=0, tiled=True)


def tie(value, *after):
    if not after:
        return value
    return lax.optimization_barrier((value, *after))[0]


def on_device(hidden, w_zx, w_dt, w_bc, dt_bias, a_log, d_skip, norm_gain, w_out, grad_out):
    rows = hidden.shape[0]
    wide = HEADS * HDIM
    rows_here = w_zx.shape[0]
    width = w_zx.shape[2]
    bc_cols = w_bc.shape[1] * w_bc.shape[2]
    nheads = w_dt.shape[1]
    n_head = lax.axis_size("head")
    quarter = bc_cols // n_head
    w_z = w_zx[:, 0]
    w_x = w_zx[:, 1]
    w_bcq = lax.dynamic_slice_in_dim(
        w_bc.reshape(rows_here, bc_cols), lax.axis_index("head") * quarter, quarter, 1
    )
    w_small = jnp.concatenate(
        [w_bcq, w_dt, jnp.zeros((rows_here, LANES - quarter - nheads), BF16)], axis=1
    )
    pad = ((0, 0), (0, LANES - nheads))
    bias = jnp.pad(dt_bias[None], pad)
    alog = jnp.pad(a_log[None], pad)
    skip = jnp.repeat(d_skip, HDIM)[None]
    gain = norm_gain[None]

    if square():
        moved = transposed(hidden)
        hid = head_gather(moved, True)
        hid = hid.reshape(-1, hid.shape[-1])
    else:
        hid = moved = to_columns(hidden)
    part_x = mm(hid, w_x).astype(BF16)
    hid_z, part_x = lax.optimization_barrier((hid, part_x))
    xr = summed_rows(part_x)
    part_z = mm(hid_z, w_z).astype(BF16)
    zr = summed_rows(part_z)

    row_blocks = feature_blocks(tie(hidden, moved))
    small_t = jnp.transpose(w_small)[: (quarter + nheads + 15) // 16 * 16]
    shards = seq_blocks(tie(small_t, moved))
    row_stack = jnp.stack(row_blocks)
    row_stack = jnp.stack(
        [lax.dynamic_index_in_dim(row_stack, at, 0, keepdims=False) for at, _ in shards]
    )
    small_stack = jnp.stack([part for _, part in shards])
    small = jnp.einsum("btd,bkd->tk", row_stack, small_stack, preferred_element_type=F32)
    small = jnp.pad(small.astype(BF16), ((0, 0), (0, LANES - small.shape[1])))
    pieces = head_gather(small) if square() else lax.all_gather(small, "head")
    bcdt = jnp.concatenate(
        [pieces[k, :, :quarter] for k in range(n_head)]
        + [jnp.pad(small[:, quarter : quarter + nheads], pad)],
        axis=1,
    )
    w_full = all_output_weights(w_out, part_z)
    gout_rows = jnp.stack(feature_blocks(tie(grad_out, part_x)))
    grad_gated = jnp.einsum("btd,bkd->tk", gout_rows, w_full, preferred_element_type=F32).astype(BF16)

    packed = ((width + EXTRA, LANES), BF16)
    flat = (rows, width)
    per_head = ((rows, LANES), F32)
    dt_val, cumul, dt_wide, cum_wide = call(steps_kernel, per_head, per_head, (flat, F32), (flat, F32))(
        bcdt, bias, alog
    )
    (local,) = call(states_kernel, packed)(xr, bcdt, cumul, dt_wide, cum_wide)
    before = shards_before(local, 1)
    (y_own,) = call(within_kernel, (flat, F32))(xr, bcdt, cumul, dt_wide, skip)
    s_in, y_val, sums = call(mixed_kernel, ((width, LANES), F32), (flat, F32), ((8, rows), F32))(
        *before, y_own, zr, bcdt, cum_wide, gain, grad_gated
    )
    sums = lax.psum(sums, "head")
    gated, d_z, grad_y, d_state, gain_part = call(
        functools.partial(norm_kernel, wide=wide),
        (flat, BF16),
        (flat, BF16),
        (flat, F32),
        packed,
        ((1, width), F32),
    )(sums, y_val, zr, bcdt, cum_wide, gain, grad_gated, local[width:])
    later = shards_before(d_state, -1)
    dx_own, dbc_own = call(back_within_kernel, (flat, F32), ((rows, bc_cols), F32))(
        xr, bcdt, cumul, dt_wide, grad_y
    )
    d_x, d_bcdt, sums_small, dskip_part = call(
        back_kernel,
        (flat, BF16),
        ((rows, bc_cols + LANES), BF16),
        ((8, LANES), F32),
        ((1, width), F32),
    )(
        *later,
        s_in,
        xr,
        bcdt,
        bias,
        alog,
        dt_val,
        cumul,
        dt_wide,
        cum_wide,
        skip,
        y_val,
        grad_y,
        dx_own,
        dbc_own,
    )

    dz_all = all_rows(d_z)
    dx_all = all_rows(d_x)
    gout = to_columns(tie(grad_out, dz_all))
    quarters = [d_bcdt[:, k * quarter : (k + 1) * quarter] for k in range(n_head)]
    if square():
        d_bcq = head_sum(jnp.stack(quarters))
    else:
        d_bcq = lax.psum_scatter(jnp.stack(quarters), "head", scatter_dimension=0)
    d_small = jnp.concatenate(
        [
            d_bcq,
            d_bcdt[:, bc_cols : bc_cols + nheads],
            jnp.zeros((rows, LANES - quarter - nheads), BF16),
        ],
        axis=1,
    )
    small_all = seq_stack(d_small)
    layer_out = sum_blocks(
        jnp.einsum("tk,bkd->btd", tie(gated, dz_all), w_full, preferred_element_type=F32).astype(BF16)
    )
    param_sums = lax.psum(
        (
            sums_small[0, :nheads],
            sums_small[1, :nheads],
            jnp.sum(dskip_part.reshape(nheads, HDIM), axis=1),
            gain_part[0],
        ),
        "seq",
    )
    grad_wz = mm(hid, dz_all, (0, 0))
    term_z = mm(dz_all, w_z, (1, 1)) + mm(small_all, w_small, (1, 1))
    grad_small = mm(hid, small_all, (0, 0))
    gated_all = all_rows(tie(gated, dx_all))
    term = (term_z + mm(dx_all, w_x, (1, 1))).astype(BF16)
    grad_hidden, reduced = from_columns(term)
    grad_wx = mm(tie(hid, reduced), dx_all, (0, 0))
    grad_wbcq = grad_small[:, :quarter].astype(BF16)
    grad_wbc = head_gather(grad_wbcq) if square() else lax.all_gather(grad_wbcq, "head")
    grad_wbc = jnp.concatenate(list(grad_wbc), axis=1).astype(F32)
    grad_wzx = jnp.stack([grad_wz, grad_wx], axis=1)
    grad_wout = mm(gated_all, gout, (0, 0))
    grad_dtbias, grad_alog, grad_dskip, grad_gain = param_sums
    return (
        layer_out,
        grad_hidden,
        grad_wzx,
        grad_small[:, quarter : quarter + nheads],
        grad_wbc.reshape(w_bc.shape),
        grad_dtbias,
        grad_alog,
        grad_dskip,
        grad_gain,
        grad_wout,
    )


def solution(mesh):
    in_specs = (
        P(("groups", "seq"), "head"),
        P("seq", None, "head"),
        P("seq", "head"),
        P("seq", None, None),
        P("head"),
        P("head"),
        P("head"),
        P("head"),
        P("head", "seq"),
        P(("groups", "seq"), "head"),
    )
    out_specs = (
        P(("groups", "seq"), "head"),
        P(("groups", "seq"), "head"),
        P(("groups", "seq"), None, "head"),
        P(("groups", "seq"), "head"),
        P(("groups", "seq"), None, None),
        P(("groups", "head")),
        P(("groups", "head")),
        P(("groups", "head")),
        P(("groups", "head")),
        P(("groups", "head"), "seq"),
    )
    return jax.shard_map(
        on_device, mesh=mesh, in_specs=in_specs, out_specs=out_specs, check_vma=False
    )
```

```python
import functools

import jax
import jax.numpy as jnp
from jax import lax
from jax.experimental import pallas as pl
from jax.experimental.pallas import tpu as pltpu
from jax.sharding import PartitionSpec as P

HEADS = 48
HDIM = 64
LANES = 128
EPS_NORM = 1e-05
HIGH = lax.Precision.HIGHEST
F32 = jnp.float32
BF16 = jnp.bfloat16
EXTRA = 16


def mm(a, b, contract=(1, 0), precision=None):
    return lax.dot_general(
        a,
        b,
        (((contract[0],), (contract[1],)), ((), ())),
        preferred_element_type=F32,
        precision=precision,
    )


def iota(shape, dim):
    return lax.broadcasted_iota(jnp.int32, shape, dim)


def spread_matrix(width):
    return (iota((LANES, width), 1) // HDIM == iota((LANES, width), 0)).astype(F32)


def spread(per_head, width):
    return mm(per_head, spread_matrix(width), precision=HIGH)


def gather_heads(values):
    return mm(values, spread_matrix(values.shape[1]), (1, 1), precision=HIGH)


def step_sizes(dtr, dt_bias, a_log):
    rows = dtr.shape[0]
    dt_val = jax.nn.softplus(dtr.astype(F32) + dt_bias)
    log_decay = -dt_val * jnp.exp(a_log)
    lower = (iota((rows, rows), 0) >= iota((rows, rows), 1)).astype(F32)
    return (dt_val, log_decay, mm(lower, log_decay, precision=HIGH))


def state_column(row, width):
    pick = iota((width, LANES), 0) // HDIM == iota((width, LANES), 1)
    return jnp.sum(jnp.where(pick, row, 0.0), axis=1, keepdims=True)


def half_masks(rows):
    low = iota((rows, LANES), 1) < HDIM
    return (low, jnp.logical_not(low))


def steps_kernel(bcdt_ref, bias_ref, alog_ref, dt_ref, cum_ref, dtw_ref, cumw_ref):
    width = dtw_ref.shape[1]
    dt_val, _, cumul = step_sizes(
        bcdt_ref[:, bcdt_ref.shape[1] - LANES :], bias_ref[...], alog_ref[...]
    )
    dt_ref[...] = dt_val
    cum_ref[...] = cumul
    dtw_ref[...] = spread(dt_val, width)
    cumw_ref[...] = spread(cumul, width)


def states_kernel(xr_ref, bcdt_ref, cum_ref, dtw_ref, cumw_ref, out_ref):
    rows, width = xr_ref.shape
    n_state = (bcdt_ref.shape[1] - LANES) // 2
    x_in = jax.nn.silu(xr_ref[...].astype(F32))
    cum_wide = cumw_ref[...]
    fade_out = jnp.exp(cum_wide[rows - 1 : rows, :] - cum_wide)
    state = mm((fade_out * dtw_ref[...] * x_in).astype(BF16), bcdt_ref[:, :n_state], (0, 0))
    out_ref[:width, :] = state.astype(BF16)
    decay = jnp.exp(cum_ref[rows - 1 : rows, :])
    upper = decay.astype(BF16)
    rest = (decay - upper.astype(F32)).astype(BF16)
    at = iota((EXTRA, LANES), 0)
    out_ref[width:, :] = jnp.where(
        at == 0, upper.astype(F32), jnp.where(at == 1, rest.astype(F32), 0.0)
    ).astype(BF16)


def within_kernel(xr_ref, bcdt_ref, cum_ref, dtw_ref, skip_ref, y_ref):
    rows, width = xr_ref.shape
    n_state = (bcdt_ref.shape[1] - LANES) // 2
    cumul = cum_ref[...]
    x_in = jax.nn.silu(xr_ref[...].astype(F32))
    x_dt = (dtw_ref[...] * x_in).astype(BF16)
    scores = mm(bcdt_ref[:, n_state : 2 * n_state], bcdt_ref[:, :n_state], (1, 1))
    seen = iota((rows, rows), 0) >= iota((rows, rows), 1)
    across = jnp.transpose(cumul)
    halves = half_masks(rows)
    for pair in range(width // LANES):
        cols = slice(pair * LANES, (pair + 1) * LANES)
        total = skip_ref[:, cols] * x_in[:, cols]
        for side in range(2):
            head = 2 * pair + side
            gaps = cumul[:, head : head + 1] - across[head : head + 1, :]
            weights = (jnp.exp(jnp.where(seen, gaps, -1e30)) * scores).astype(BF16)
            total = total + mm(weights, jnp.where(halves[side], x_dt[:, cols], 0))
        y_ref[:, cols] = total


def fold(from_far, width):
    state = from_far[0][:width, :].astype(F32)
    for part in from_far[1:]:
        decay = state_column(
            part[width : width + 1, :].astype(F32) + part[width + 1 : width + 2, :].astype(F32), width
        )
        state = decay * state + part[:width, :].astype(F32)
    return state


def hop_kernel(packed_ref, got_ref, out_ref):
    width = out_ref.shape[0]
    own = packed_ref[:width, :].astype(F32)
    decay = packed_ref[width : width + 1, :].astype(F32) + packed_ref[width + 1 : width + 2, :].astype(F32)
    out_ref[...] = (state_column(decay, width) * got_ref[:width, :].astype(F32) + own).astype(BF16)


def mixed_kernel(*refs):
    parts = refs[:-9]
    y_ref, z_ref, bcdt_ref, cumw_ref, gain_ref, gg_ref, s_ref, out_ref, sums_ref = refs[-9:]
    rows, width = y_ref.shape
    n_state = (bcdt_ref.shape[1] - LANES) // 2
    state = fold([part[...] for part in parts], width)
    s_ref[...] = state
    flow = mm(bcdt_ref[:, n_state : 2 * n_state], state.astype(BF16), (1, 1))
    y_val = y_ref[...] + flow * jnp.exp(cumw_ref[...])
    out_ref[...] = y_val
    mixed = y_val * jax.nn.silu(z_ref[...].astype(F32))
    squares = jnp.sum(mixed * mixed, axis=1, keepdims=True)
    inner = jnp.sum(gg_ref[...].astype(F32) * gain_ref[...] * mixed, axis=1, keepdims=True)
    at = iota((rows, LANES), 1)
    sums = jnp.where(at == 0, squares, jnp.where(at == 1, inner, 0.0))
    sums_ref[...] = jnp.transpose(sums)[:8]


def norm_kernel(
    sums_ref, y_ref, z_ref, bcdt_ref, cumw_ref, gain_ref, gg_ref, decay_ref,
    gated_ref, dz_ref, gy_ref, ds_ref, gg_out_ref, *, wide
):
    rows, width = y_ref.shape
    n_state = (bcdt_ref.shape[1] - LANES) // 2
    sums = jnp.transpose(sums_ref[...])
    rinv = lax.rsqrt(sums[:, 0:1] / wide + EPS_NORM)
    inner = sums[:, 1:2]
    z_val = z_ref[...].astype(F32)
    sig = jax.nn.sigmoid(z_val)
    gate = z_val * sig
    y_val = y_ref[...]
    mixed = y_val * gate
    upstream = gg_ref[...].astype(F32)
    gain = gain_ref[...]
    normed = mixed * rinv
    gated_ref[...] = (normed * gain).astype(BF16)
    gg_out_ref[...] = jnp.sum(upstream * normed, axis=0, keepdims=True)
    grad_mixed = rinv * gain * upstream - mixed * (rinv * rinv * rinv * inner / wide)
    dz_ref[...] = (grad_mixed * y_val * (sig * (1.0 + z_val * (1.0 - sig)))).astype(BF16)
    grad_y = grad_mixed * gate
    gy_ref[...] = grad_y
    flow = (grad_y * jnp.exp(cumw_ref[...])).astype(BF16)
    ds_ref[:width, :] = mm(flow, bcdt_ref[:, n_state : 2 * n_state], (0, 0)).astype(BF16)
    ds_ref[width:, :] = decay_ref[...]


def back_within_kernel(xr_ref, bcdt_ref, cum_ref, dtw_ref, gy_ref, dx_ref, dbc_ref):
    rows, width = xr_ref.shape
    n_state = (bcdt_ref.shape[1] - LANES) // 2
    cumul = cum_ref[...]
    x_in = jax.nn.silu(xr_ref[...].astype(F32))
    x_dt = (dtw_ref[...] * x_in).astype(BF16)
    grad_y = gy_ref[...].astype(BF16)
    b_in = bcdt_ref[:, :n_state]
    c_in = bcdt_ref[:, n_state : 2 * n_state]
    scores = mm(b_in, c_in, (1, 1))
    seen = iota((rows, rows), 1) >= iota((rows, rows), 0)
    across = jnp.transpose(cumul)
    halves = half_masks(rows)
    d_scores = jnp.zeros((rows, rows), F32)
    for pair in range(width // LANES):
        cols = slice(pair * LANES, (pair + 1) * LANES)
        total = jnp.zeros((rows, LANES), F32)
        for side in range(2):
            head = 2 * pair + side
            gaps = across[head : head + 1, :] - cumul[:, head : head + 1]
            fade = jnp.exp(jnp.where(seen, gaps, -1e30))
            total = total + mm(
                (fade * scores).astype(BF16), jnp.where(halves[side], grad_y[:, cols], 0)
            )
            d_scores = d_scores + fade * mm(
                jnp.where(halves[side], x_dt[:, cols], 0), grad_y[:, cols], (1, 1)
            )
        dx_ref[:, cols] = total
    d_scores = d_scores.astype(BF16)
    dbc_ref[:, :n_state] = mm(d_scores, c_in)
    dbc_ref[:, n_state:] = mm(d_scores, b_in, (0, 0))


def back_kernel(*refs):
    parts = refs[:-18]
    s_ref, xr_ref, bcdt_ref, bias_ref, alog_ref, dt_ref, cum_ref, dtw_ref, cumw_ref = refs[-18:-9]
    skip_ref, y_ref, gy_ref, dxw_ref, dbcw_ref = refs[-9:-4]
    dx_ref, dbc_ref, small_ref, dskip_ref = refs[-4:]
    rows, width = xr_ref.shape
    n_state = (bcdt_ref.shape[1] - LANES) // 2
    dtr = bcdt_ref[:, 2 * n_state :].astype(F32)
    dt_val = dt_ref[...]
    rate = jnp.exp(alog_ref[...])
    tail = cum_ref[rows - 1 : rows, :]
    b_in = bcdt_ref[:, :n_state]
    state = s_ref[...]
    later = fold([part[...] for part in parts], width)
    later_b = later.astype(BF16)
    raw = xr_ref[...].astype(F32)
    sig = jax.nn.sigmoid(raw)
    x_in = raw * sig
    cum_wide = cumw_ref[...]
    fade_out = jnp.exp(cum_wide[rows - 1 : rows, :] - cum_wide)
    dt_wide = dtw_ref[...]
    grad_y = gy_ref[...]
    skip = skip_ref[...]
    flow = fade_out * mm(b_in, later_b, (1, 1))
    d_xdt = dxw_ref[...] + flow
    x_dt = (dt_wide * x_in).astype(BF16).astype(F32)
    grad_r = grad_y.astype(BF16).astype(F32)
    d_x = dt_wide * d_xdt + skip * grad_y
    dx_ref[...] = (d_x * (sig * (1.0 + raw * (1.0 - sig)))).astype(BF16)
    d_dt = gather_heads(x_in * d_xdt)
    moved = gather_heads(grad_r * (y_ref[...] - skip * x_in) - x_dt * d_xdt)
    tail_part = jnp.sum(gather_heads(x_dt * flow), axis=0, keepdims=True)
    pairs = jnp.sum(later * state, axis=1, keepdims=True)
    pick = iota((width, LANES), 0) // HDIM == iota((width, LANES), 1)
    state_part = jnp.sum(jnp.where(pick, pairs, 0.0), axis=0, keepdims=True) * jnp.exp(tail)
    upper = (iota((rows, rows), 1) >= iota((rows, rows), 0)).astype(F32)
    d_log = mm(upper, moved, precision=HIGH) + tail_part + state_part
    d_dt = d_dt - rate * d_log
    d_dtr = d_dt * jax.nn.sigmoid(dtr + bias_ref[...])
    at = iota((8, LANES), 0)
    d_bias = jnp.sum(d_dtr, axis=0, keepdims=True)
    d_alog = jnp.sum(d_log * (-dt_val * rate), axis=0, keepdims=True)
    small_ref[...] = jnp.where(at == 0, d_bias, jnp.where(at == 1, d_alog, 0.0))
    dskip_ref[...] = jnp.sum(grad_y * x_in, axis=0, keepdims=True)
    inflow = (fade_out * x_dt).astype(BF16)
    dbc_ref[:, :n_state] = (dbcw_ref[:, :n_state] + mm(inflow, later_b)).astype(BF16)
    outflow = (grad_y * jnp.exp(cum_wide)).astype(BF16)
    dbc_ref[:, n_state : 2 * n_state] = (
        dbcw_ref[:, n_state:] + mm(outflow, state.astype(BF16))
    ).astype(BF16)
    dbc_ref[:, 2 * n_state :] = d_dtr.astype(BF16)


def call(kernel, *outs):
    def run(*args):
        vmem = pl.BlockSpec(memory_space=pltpu.VMEM)
        return pl.pallas_call(
            kernel,
            out_shape=[jax.ShapeDtypeStruct(*o) for o in outs],
            in_specs=[vmem] * len(args),
            out_specs=[vmem] * len(outs),
            compiler_params=pltpu.CompilerParams(vmem_limit_bytes=48 * 1024 * 1024),
        )(*args)

    return run


def square():
    return lax.axis_size("seq") == 4 and lax.axis_size("head") == 4


def exchange(tile, bit):
    return lax.ppermute(tile, "head", [(h, h ^ bit) for h in range(lax.axis_size("head"))])


def lanes():
    me, here = (lax.axis_index("head"), lax.axis_index("seq"))
    return (me // 2, me % 2, here // 2, here % 2)


def head_gather(tile, crossed=False):
    chip, core, high, low = lanes()
    if crossed:
        chip, core = (chip ^ low, core ^ high)
    other = exchange(tile, 2)
    mine = jnp.stack([jnp.where(chip == 0, tile, other), jnp.where(chip == 0, other, tile)])
    across = exchange(mine, 1)
    first, second = (jnp.where(core == 0, mine, across), jnp.where(core == 0, across, mine))
    if crossed:
        return jnp.concatenate([first, second])
    return jnp.stack([first[0], second[0], first[1], second[1]])


def head_sum(parts, crossed=False):
    chip, core, high, low = lanes()
    if crossed:
        chip, core = (chip ^ low, core ^ high)
        zero, one = (parts[:2], parts[2:])
    else:
        zero, one = (parts[0::2], parts[1::2])
    got = exchange(jnp.where(core == 0, one, zero), 1)
    half = (jnp.where(core == 0, zero, one).astype(F32) + got.astype(F32)).astype(BF16)
    got = exchange(jnp.where(chip == 0, half[1], half[0]), 2)
    return (jnp.where(chip == 0, half[0], half[1]).astype(F32) + got.astype(F32)).astype(BF16)


BIT_SWAP = (0, 2, 1, 3)


def transposed(tile):
    out = [(s * 4 + h, s * 4 + BIT_SWAP[s ^ h]) for s in range(4) for h in range(4)]
    over = [(s * 4 + BIT_SWAP[s ^ h], h * 4 + BIT_SWAP[s ^ h]) for s in range(4) for h in range(4)]
    return lax.ppermute(lax.ppermute(tile, ("seq", "head"), out), ("seq", "head"), over)


def transposed_back(tile):
    pairs = [(s * 4 + BIT_SWAP[q ^ s], q * 4 + s) for s in range(4) for q in range(4)]
    return lax.ppermute(tile, ("seq", "head"), pairs)


def to_columns(tile):
    if square():
        stacked = head_gather(transposed(tile), True)
        return stacked.reshape(-1, stacked.shape[-1])
    rows = lax.all_gather(tile, "head", axis=1, tiled=True)
    return lax.all_to_all(rows, "seq", split_axis=1, concat_axis=0, tiled=True)


def from_columns(partial_value):
    if square():
        reduced = head_sum(partial_value.reshape(4, -1, partial_value.shape[-1]), True)
        return (transposed_back(reduced), reduced)
    rows = lax.all_to_all(partial_value, "seq", split_axis=0, concat_axis=1, tiled=True)
    reduced = lax.psum_scatter(rows, "head", scatter_dimension=1, tiled=True)
    return (reduced, reduced)


def feature_blocks(tile):
    if square():
        return list(head_gather(tile))
    return jnp.split(lax.all_gather(tile, "head", axis=1, tiled=True), lax.axis_size("seq"), axis=1)


def sum_blocks(blocks):
    if square():
        return head_sum(blocks)
    return lax.psum_scatter(jnp.concatenate(list(blocks), axis=1), "head", scatter_dimension=1, tiled=True)


def shards_before(packed, step):
    n_seq = lax.axis_size("seq")
    if n_seq == 4 and step < 0:
        return [
            lax.ppermute(packed, "seq", [(s, s - k) for s in range(k, n_seq)])
            for k in range(n_seq - 1, 0, -1)
        ]
    if n_seq == 4:
        width = packed.shape[0] - EXTRA
        near = lax.ppermute(packed, "seq", [(s, s + step) for s in range(4) if 0 <= s + step < 4])
        (both,) = call(hop_kernel, ((width, LANES), BF16))(packed, near)
        far = lax.ppermute(both, "seq", [(s, s + 2 * step) for s in range(4) if 0 <= s + 2 * step < 4])
        return [far, near]
    everything = lax.all_gather(packed, "seq")
    here = lax.axis_index("seq")
    parts = []
    for k in range(n_seq - 1, 0, -1):
        at = here - k * step
        part = lax.dynamic_index_in_dim(everything, jnp.clip(at, 0, n_seq - 1), 0, keepdims=False)
        parts.append(jnp.where((at >= 0) & (at < n_seq), part, 0))
    return parts


def all_output_weights(w_out, after):
    groups = lax.axis_size("groups")
    if groups != 2:
        return lax.all_gather(w_out, "seq")
    me = lax.axis_index("groups")
    half = w_out.shape[0] // 2
    part = lax.dynamic_slice_in_dim(w_out, me * half, half, 0)
    mine = lax.all_gather(part, "seq")
    other = lax.ppermute(tie(mine, after), "groups", [(0, 1), (1, 0)])
    return jnp.concatenate(
        [jnp.where(me == 0, mine, other), jnp.where(me == 0, other, mine)], axis=1
    )


def seq_blocks(value):
    n_seq = lax.axis_size("seq")
    if n_seq > 4:
        return list(enumerate(lax.all_gather(value, "seq")))
    here = lax.axis_index("seq")
    shards = [(here, value)]
    for k in range(1, n_seq):
        moved = lax.ppermute(value, "seq", [(s, (s + k) % n_seq) for s in range(n_seq)])
        shards.append(((here - k) % n_seq, moved))
    return shards


def seq_stack(value):
    n_seq = lax.axis_size("seq")
    shards = seq_blocks(value)
    if n_seq > 4:
        return jnp.concatenate([part for _, part in shards])
    stacked = jnp.stack([part for _, part in shards])
    here = lax.axis_index("seq")
    return jnp.concatenate(
        [
            lax.dynamic_index_in_dim(stacked, (here - j) % n_seq, 0, keepdims=False)
            for j in range(n_seq)
        ]
    )


def summed_rows(partial_value):
    return lax.psum_scatter(partial_value.astype(BF16), "seq", scatter_dimension=0, tiled=True)


def all_rows(value):
    return lax.all_gather(value, "seq", axis=0, tiled=True)


def tie(value, *after):
    if not after:
        return value
    return lax.optimization_barrier((value, *after))[0]


def on_device(hidden, w_zx, w_dt, w_bc, dt_bias, a_log, d_skip, norm_gain, w_out, grad_out):
    rows = hidden.shape[0]
    wide = HEADS * HDIM
    rows_here = w_zx.shape[0]
    width = w_zx.shape[2]
    bc_cols = w_bc.shape[1] * w_bc.shape[2]
    nheads = w_dt.shape[1]
    n_head = lax.axis_size("head")
    quarter = bc_cols // n_head
    w_z = w_zx[:, 0]
    w_x = w_zx[:, 1]
    w_bcq = lax.dynamic_slice_in_dim(
        w_bc.reshape(rows_here, bc_cols), lax.axis_index("head") * quarter, quarter, 1
    )
    w_small = jnp.concatenate(
        [w_bcq, w_dt, jnp.zeros((rows_here, LANES - quarter - nheads), BF16)], axis=1
    )
    pad = ((0, 0), (0, LANES - nheads))
    bias = jnp.pad(dt_bias[None], pad)
    alog = jnp.pad(a_log[None], pad)
    skip = jnp.repeat(d_skip, HDIM)[None]
    gain = norm_gain[None]

    if square():
        moved = transposed(hidden)
        hid = head_gather(moved, True)
        hid = hid.reshape(-1, hid.shape[-1])
    else:
        hid = moved = to_columns(hidden)
    part_x = mm(hid, w_x).astype(BF16)
    hid_z, part_x = lax.optimization_barrier((hid, part_x))
    xr = summed_rows(part_x)
    part_z = mm(hid_z, w_z).astype(BF16)
    zr = summed_rows(part_z)

    row_blocks = feature_blocks(tie(hidden, moved))
    small_t = jnp.transpose(w_small)[: (quarter + nheads + 15) // 16 * 16]
    shards = seq_blocks(tie(small_t, moved))
    row_stack = jnp.stack(row_blocks)
    row_stack = jnp.stack(
        [lax.dynamic_index_in_dim(row_stack, at, 0, keepdims=False) for at, _ in shards]
    )
    small_stack = jnp.stack([part for _, part in shards])
    small = jnp.einsum("btd,bkd->tk", row_stack, small_stack, preferred_element_type=F32)
    small = jnp.pad(small.astype(BF16), ((0, 0), (0, LANES - small.shape[1])))
    pieces = head_gather(small) if square() else lax.all_gather(small, "head")
    bcdt = jnp.concatenate(
        [pieces[k, :, :quarter] for k in range(n_head)]
        + [jnp.pad(small[:, quarter : quarter + nheads], pad)],
        axis=1,
    )
    w_full = all_output_weights(w_out, part_z)
    gout_rows = jnp.stack(feature_blocks(tie(grad_out, part_x)))
    grad_gated = jnp.einsum("btd,bkd->tk", gout_rows, w_full, preferred_element_type=F32).astype(BF16)

    packed = ((width + EXTRA, LANES), BF16)
    flat = (rows, width)
    per_head = ((rows, LANES), F32)
    dt_val, cumul, dt_wide, cum_wide = call(steps_kernel, per_head, per_head, (flat, F32), (flat, F32))(
        bcdt, bias, alog
    )
    (local,) = call(states_kernel, packed)(xr, bcdt, cumul, dt_wide, cum_wide)
    before = shards_before(local, 1)
    (y_own,) = call(within_kernel, (flat, F32))(xr, bcdt, cumul, dt_wide, skip)
    s_in, y_val, sums = call(mixed_kernel, ((width, LANES), F32), (flat, F32), ((8, rows), F32))(
        *before, y_own, zr, bcdt, cum_wide, gain, grad_gated
    )
    sums = lax.psum(sums, "head")
    gated, d_z, grad_y, d_state, gain_part = call(
        functools.partial(norm_kernel, wide=wide),
        (flat, BF16),
        (flat, BF16),
        (flat, F32),
        packed,
        ((1, width), F32),
    )(sums, y_val, zr, bcdt, cum_wide, gain, grad_gated, local[width:])
    later = shards_before(d_state, -1)
    dx_own, dbc_own = call(back_within_kernel, (flat, F32), ((rows, bc_cols), F32))(
        xr, bcdt, cumul, dt_wide, grad_y
    )
    d_x, d_bcdt, sums_small, dskip_part = call(
        back_kernel,
        (flat, BF16),
        ((rows, bc_cols + LANES), BF16),
        ((8, LANES), F32),
        ((1, width), F32),
    )(
        *later,
        s_in,
        xr,
        bcdt,
        bias,
        alog,
        dt_val,
        cumul,
        dt_wide,
        cum_wide,
        skip,
        y_val,
        grad_y,
        dx_own,
        dbc_own,
    )

    dz_all = all_rows(d_z)
    dx_all = all_rows(d_x)
    gout = to_columns(tie(grad_out, dz_all))
    quarters = [d_bcdt[:, k * quarter : (k + 1) * quarter] for k in range(n_head)]
    if square():
        d_bcq = head_sum(jnp.stack(quarters))
    else:
        d_bcq = lax.psum_scatter(jnp.stack(quarters), "head", scatter_dimension=0)
    d_small = jnp.concatenate(
        [
            d_bcq,
            d_bcdt[:, bc_cols : bc_cols + nheads],
            jnp.zeros((rows, LANES - quarter - nheads), BF16),
        ],
        axis=1,
    )
    small_all = seq_stack(d_small)
    layer_out = sum_blocks(
        jnp.einsum("tk,bkd->btd", tie(gated, dz_all), w_full, preferred_element_type=F32).astype(BF16)
    )
    param_sums = lax.psum(
        (
            sums_small[0, :nheads],
            sums_small[1, :nheads],
            jnp.sum(dskip_part.reshape(nheads, HDIM), axis=1),
            gain_part[0],
        ),
        "seq",
    )
    grad_wz = mm(hid, dz_all, (0, 0))
    term_z = mm(dz_all, w_z, (1, 1)) + mm(small_all, w_small, (1, 1))
    grad_small = mm(hid, small_all, (0, 0))
    gated_all = all_rows(tie(gated, dx_all))
    term = (term_z + mm(dx_all, w_x, (1, 1))).astype(BF16)
    grad_hidden, reduced = from_columns(term)
    grad_wx = mm(tie(hid, reduced), dx_all, (0, 0))
    grad_wbcq = grad_small[:, :quarter].astype(BF16)
    grad_wbc = head_gather(grad_wbcq) if square() else lax.all_gather(grad_wbcq, "head")
    grad_wbc = jnp.concatenate(list(grad_wbc), axis=1).astype(F32)
    grad_wzx = jnp.stack([grad_wz, grad_wx], axis=1)
    grad_wout = mm(gated_all, gout, (0, 0))
    grad_dtbias, grad_alog, grad_dskip, grad_gain = param_sums
    return (
        layer_out,
        grad_hidden,
        grad_wzx,
        grad_small[:, quarter : quarter + nheads],
        grad_wbc.reshape(w_bc.shape),
        grad_dtbias,
        grad_alog,
        grad_dskip,
        grad_gain,
        grad_wout,
    )


def solution(mesh):
    in_specs = (
        P(("groups", "seq"), "head"),
        P("seq", None, "head"),
        P("seq", "head"),
        P("seq", None, None),
        P("head"),
        P("head"),
        P("head"),
        P("head"),
        P("head", "seq"),
        P(("groups", "seq"), "head"),
    )
    out_specs = (
        P(("groups", "seq"), "head"),
        P(("groups", "seq"), "head"),
        P(("groups", "seq"), None, "head"),
        P(("groups", "seq"), "head"),
        P(("groups", "seq"), None, None),
        P(("groups", "head")),
        P(("groups", "head")),
        P(("groups", "head")),
        P(("groups", "head")),
        P(("groups", "head"), "seq"),
    )
    return jax.shard_map(
        on_device, mesh=mesh, in_specs=in_specs, out_specs=out_specs, check_vma=False
    )
```
